32 devices in a mesh: patch: 16 (over z, y, core), lag: 2 (over x).
Axes of the slice: x: 2, y: 2, z: 4, core: 2. Of those that a mesh axis runs over, the one named last changes fastest.
Arguments:
- interaction: bfloat16 [30, 4096, 1280], P('lag', 'patch'), may hold values from -0.046875 to 0.046875
- history: bfloat16 [30, 4096, 128], P('lag', 'patch'), may hold values from -6 to 6
- near_inverse: bfloat16 [4096, 256], P('patch'), may hold values from -0.375 to 0.375
- lag_ranges: int32 [16, 10], P('patch'), may hold values from 1 to 31, as said below
- receiver_tile: int32 [4096, 1], P('patch'), may hold values from 0 to 15; in each aligned block of 256 rows (0 to 255, 256 to 511, ...) at most 16 rows name the same one
- receiver_panel: int32 [4096], P('patch'), may hold values from 0 to 255
- residuals: bfloat16 [4096, 4, 128], P('patch'), may hold values from -6 to 6
Outputs:
- densities: bfloat16 [4, 4096, 128], P(None, 'patch')
The draws below stay inside these ranges and needn't reach their ends.
Inputs may be any that keep to these rules, and one draw needn't show every extreme that they name: `lag_ranges`: columns 0 to 4 hold the first active lag, columns 5 to 9 one past the last; every range holds at least 7 lags. `receiver_tile`: among the 256 receivers of one patch index, at most 16 lie on one patch.
All inputs are finite; a program needn't handle non-finite values.
Results may differ from the reference program's by a relative error of at most 0.0049.
Values may be sent and summed in bfloat16 or wider, within the bound.
No kernel may reach another device: no remote copies, remote signals or barrier semaphores. Data moves between devices by JAX's collectives and lax.ppermute only.
A program may use at most 64 MiB of HBM per device.

```python
import math
import jax
import jax.numpy as jnp
import numpy as np
from jax import lax

TILE = 256
NEAR = 5
STEPS = 4
SHOTS = 128
RECV_DEV = 256
CAP = 16
TILES = 16
PANELS = 4096
LAGS = 30
RECEIVERS = 4096


def draw_lag_ranges(key, part):
    key_lower, key_count = jax.random.split(jax.random.fold_in(key, 7))
    lower = jax.random.randint(key_lower, (TILES, NEAR), 1, LAGS // 2 + 2)
    counts = jax.random.randint(key_count, (TILES, NEAR), LAGS // 4, LAGS // 2 + 1)
    return jnp.concatenate([lower, lower + counts], 1).astype(jnp.int32)


def plant(array, key, smallest, high):
    shape = array.shape
    index_at = [jax.random.randint(jax.random.fold_in(key, axis), (), 0, shape[axis]) for axis in range(len(shape))]
    array = array.at[tuple(index_at)].set(smallest)
    longest = shape.index(max(shape))
    index_at[longest] = (index_at[longest] + 1) % shape[longest]
    return array.at[tuple(index_at)].set(high)


def shard_levels(key, extent, cuts, least, top_value):
    level, own = 1.0, jax.random.fold_in(key, 6)
    for axis_at, shards_of in cuts:
        heights = jnp.exp(jax.random.uniform(jax.random.fold_in(own, axis_at), (shards_of,), jnp.float32, least / len(cuts), top_value / len(cuts)))
        level = level * jnp.repeat(heights, extent[axis_at] // shards_of).reshape([-1 if axis == axis_at else 1 for axis in range(len(extent))])
    return level


def assign_block(key, own, number, rows, amount, top, bound, lean):
    sequence = jax.random.permutation(key, amount)
    crowded, usual = shares(amount, rows * top, bound, lean, True), shares(amount, rows * top, bound, lean, False)
    places = jnp.arange(amount)

    def named(sizes, turn):
        used = int((sizes > 0).sum())
        fixed = max(1, used // 4)
        moved = fixed + (places - fixed + turn * (used - fixed)) % max(1, amount - fixed)
        return jnp.zeros((amount,), jnp.int32).at[sequence[jnp.where(places < fixed, places, moved)]].set(jnp.asarray(sizes, jnp.int32))

    sizes = jnp.where(number % 4 == 0, named(crowded, number // 4), named(usual, number - number // 4 - 1))
    mixed = jax.random.permutation(jax.random.fold_in(own, 3), amount)
    giver, taker = mixed[0:amount // 2 * 2:2], mixed[1:amount // 2 * 2:2]
    margin = jnp.minimum(sizes[giver] - 1, bound - sizes[taker]) // 2
    margin = jnp.where((giver == sequence[0]) | (taker == sequence[0]) | (sizes[taker] == 0), 0, jnp.maximum(margin, 0))
    moved = jax.random.randint(jax.random.fold_in(own, 4), (amount // 2,), 0, 1 << 20) % (margin + 1)
    sizes = sizes.at[giver].add(-moved).at[taker].add(moved)
    labels = jnp.searchsorted(jnp.cumsum(sizes), jnp.arange(rows * top), side="right").astype(jnp.int32)
    table = labels.reshape(top, rows).T
    table = table[jax.random.permutation(jax.random.fold_in(own, 1), rows)]
    turn = jax.random.randint(jax.random.fold_in(own, 2), (rows, 1), 0, top)
    return jnp.take_along_axis(table, (jnp.arange(top)[None, :] + turn) % top, axis=1)


def shares(count, total, limit, slope, full):
    portions = [(1 << 20) // math.isqrt(grade ** slope) + 1 for grade in range(1, count + 1)]
    largest = limit if full else min(limit, max(-(-total // count), total * portions[0] // sum(portions)))
    least = 1 if total - largest >= count - 1 else 0
    given, rest = [largest] + [least] * (count - 1), total - largest - least * (count - 1)
    while rest > 0:
        movable = [i for i in range(1, count) if given[i] < largest] or [i for i in range(1, count) if given[i] < limit]
        mass, budget = sum([portions[i] for i in movable]), rest
        for i in movable:
            addition = min(limit - given[i], max(1, budget * portions[i] // mass), rest)
            given[i] = given[i] + addition
            rest = rest - addition
    return np.array(given)


def normal_values(rng, extent, deviation, bound, pieces=(), kind=jnp.bfloat16):
    array = jax.random.normal(rng, extent, jnp.float32) * deviation
    if len(pieces) > 0:
        array = shard_levels(rng, extent, pieces, -0.22, 0.18) * array
    return jnp.clip(array, min=-bound, max=bound).astype(kind)


def setup_inputs(seed: int = 0) -> dict:
    key_of = jax.random.split(jax.random.key(seed), 8)
    interaction = normal_values(key_of[0], (LAGS, PANELS, NEAR * TILE), (3 * LAGS * NEAR * TILE // 8) ** -0.5, 0.046875, ((0, 2), (1, 16)))
    history = normal_values(key_of[1], (LAGS, PANELS, SHOTS), 1.0, 6.0, ((0, 2), (1, 16)))
    near_inverse = normal_values(key_of[2], (PANELS, TILE), TILE ** -0.5, 0.375, ((0, 16),))
    lag_ranges = draw_lag_ranges(jax.random.fold_in(key_of[7], 71), 0)
    receiver_tile_keys = jax.random.split(jax.random.fold_in(key_of[4], 1), RECEIVERS // RECV_DEV)
    receiver_tile_turns = jax.random.permutation(jax.random.fold_in(key_of[4], 3), RECEIVERS // RECV_DEV)
    receiver_tile = jax.vmap(lambda own, number: assign_block(jax.random.fold_in(key_of[4], 2), own, number, RECV_DEV, TILES, 1, CAP, 2))(receiver_tile_keys, receiver_tile_turns).reshape((RECEIVERS, 1))
    receiver_panel = plant(jax.random.randint(key_of[5], (RECEIVERS,), 0, TILE), jax.random.fold_in(key_of[5], 1), 0, TILE - 1).astype(jnp.int32)
    residuals = normal_values(key_of[6], (RECEIVERS, STEPS, SHOTS), 1.0, 6.0, ((0, 16),))
    return {"interaction": interaction, "history": history, "near_inverse": near_inverse, "lag_ranges": lag_ranges, "receiver_tile": receiver_tile, "receiver_panel": receiver_panel, "residuals": residuals}


def reference(interaction, history, near_inverse, lag_ranges, receiver_tile, receiver_panel, residuals):
    half_near = NEAR // 2
    target = (receiver_tile[:, 0] * TILE + receiver_panel).astype(jnp.int32)
    source = jax.ops.segment_sum(residuals.astype(jnp.float32), target, num_segments=PANELS)
    lag_numbers = jnp.arange(1, LAGS + 1, dtype=jnp.int32)
    lower = lag_ranges[:, :NEAR]
    upper = lag_ranges[:, NEAR:]
    active = ((lag_numbers[:, None, None] >= lower[None]) & (lag_numbers[:, None, None] < upper[None])).astype(jnp.float32)
    blocks = interaction.reshape(LAGS, TILES, TILE, NEAR, TILE)
    inverse = near_inverse.reshape(TILES, TILE, TILE).astype(jnp.float32)
    results = []
    for step_idx in range(STEPS):
        older = history[:LAGS - step_idx]
        if step_idx > 0:
            window = jnp.concatenate([jnp.stack(results[::-1]), older], 0)
        else:
            window = older

        def add_lag(totals, inputs):
            lag_block, lag_rows, lag_mask = inputs
            terms = jnp.einsum("prot,prs->pots", lag_block.astype(jnp.float32),
                               lag_rows.reshape(TILES, TILE, SHOTS).astype(jnp.float32))
            return totals + terms * lag_mask[:, :, None, None], None

        zeros_init = jnp.zeros((TILES, NEAR, TILE, SHOTS), jnp.float32)
        totals, _ = lax.scan(add_lag, zeros_init, (blocks, window, active))
        incoming = jnp.zeros((TILES, TILE, SHOTS), jnp.float32)
        for offset in range(NEAR):
            incoming = incoming + jnp.roll(totals[:, offset], offset - half_near, axis=0)
        right = (source[:, step_idx].reshape(TILES, TILE, SHOTS) - incoming).astype(jnp.bfloat16)
        density = jnp.einsum("prc,prs->pcs", inverse, right.astype(jnp.float32))
        results.append(density.astype(jnp.bfloat16).reshape(PANELS, SHOTS))
    return jnp.stack(results)
```

```python
import functools

import jax
import jax.numpy as jnp
from jax import lax
from jax.experimental import pallas as pl
from jax.experimental.pallas import tpu as pltpu
from jax.sharding import PartitionSpec as P

NEAR = 5
CAP = 16
HALF = NEAR // 2
LANES = 128
VMEM = pltpu.VMEM


def dot(left, right):
    return jnp.dot(left, right, preferred_element_type=jnp.float32)


def slot_offsets(patch):
    odd = lax.rem(patch, 2)
    high = lax.rem(lax.div(patch, 2), 2)
    return [4 * high, 1 + 2 * odd, 4 - 4 * high, 3 - 2 * odd, HALF]


def pairings(patches):
    far = [(i + 2 if i & 2 else i - 2) % patches for i in range(patches)]
    odd_even = [(i + 1 if i & 1 else i - 1) % patches for i in range(patches)]
    near = [i ^ 2 for i in range(patches)]
    core = [i ^ 1 for i in range(patches)]
    return [list(enumerate(p)) for p in (far, odd_even, near, core)]


def pack_kernel(tile_ref, panel_ref, rows_ref, out_ref):
    recv = rows_ref.shape[0]
    width = rows_ref.shape[1]
    slots = out_ref.shape[0]
    patches = slots // CAP
    tile = tile_ref[...]
    hot = lax.broadcasted_iota(jnp.int32, (patches, recv), 0) == tile
    before = lax.broadcasted_iota(jnp.int32, (recv, recv), 0) < lax.broadcasted_iota(
        jnp.int32, (recv, recv), 1
    )
    hot = jnp.where(hot, 1.0, 0.0)
    ahead = dot(hot.astype(jnp.bfloat16), jnp.where(before, 1.0, 0.0).astype(jnp.bfloat16))
    earlier = jnp.sum(hot * ahead, axis=0, keepdims=True).astype(jnp.int32)
    slot = tile * CAP + earlier
    placed = lax.broadcasted_iota(jnp.int32, (slots, recv), 0) == slot
    placer = jnp.where(placed, 1.0, 0.0).astype(jnp.bfloat16)
    out_ref[:, :width] = dot(placer, rows_ref[...]).astype(jnp.bfloat16)
    marks = jnp.where(placed, (panel_ref[...] + 1).astype(jnp.float32), 0.0)
    label = jnp.sum(marks, axis=1, keepdims=True)
    out_ref[:, width:] = jnp.broadcast_to(label, (slots, LANES)).astype(jnp.bfloat16)


def source_kernel(arrived_ref, out_ref):
    slots = arrived_ref.shape[0]
    width, tile_len = out_ref.shape
    label = arrived_ref[:, width:].astype(jnp.float32)
    lane = lax.broadcasted_iota(jnp.int32, (slots, LANES), 1)
    picker = jnp.concatenate(
        [
            jnp.where(label == (lane + (1 + first)).astype(jnp.float32), 1.0, 0.0)
            for first in range(0, tile_len, LANES)
        ],
        axis=1,
    ).astype(jnp.bfloat16)
    out_ref[...] = lax.dot_general(
        arrived_ref[:, :width],
        picker,
        (((0,), (0,)), ((), ())),
        preferred_element_type=jnp.float32,
    )


def older_kernel(steps, ranges, rim, history, weights, *refs):
    outs, (rows, blocks, total, sems) = refs[:-4], refs[-4:]
    messages, own, rest = outs[: NEAR - 1], outs[NEAR - 1], outs[NEAR:]
    band, tile_len, shots = history.shape
    lag = lax.axis_index("lag")
    offsets = slot_offsets(lax.axis_index("patch"))

    def bounds(offset):
        base = lag * band + 1
        first = jnp.clip(ranges[0, offset] - base, 0, band)
        last = jnp.clip(ranges[0, NEAR + offset] - base, 0, band)
        return first, last

    def fetch(slot, offset, k):
        columns = pl.ds(pl.multiple_of(offset * tile_len, tile_len), tile_len)
        return pltpu.make_async_copy(
            weights.at[k, :, columns], blocks.at[slot, k], sems.at[slot, k]
        )

    for slot, offset in enumerate(offsets):
        first, last = bounds(offset)
        lax.fori_loop(first, last, lambda k, c, s=slot, o=offset: fetch(s, o, k).start(), None)
    for k in range(band):
        rows[(band - 1 - k) * shots : (band - k) * shots, :] = history[k].T

    @pl.when(lag > 0)
    def _():
        for k in range(steps - 1):
            at = (band + steps - 2 - k) * shots
            rows[at : at + shots, :] = rim[k].T

    @pl.when(lag == 0)
    def _():
        rows[band * shots :, :] = jnp.zeros(((steps - 1) * shots, tile_len), jnp.bfloat16)

    for slot, offset in enumerate(offsets):
        first, last = bounds(offset)
        total[...] = jnp.zeros_like(total)

        def add(k, carry, slot=slot, offset=offset):
            fetch(slot, offset, k).wait()
            window = pl.ds(pl.multiple_of((band - 1 - k) * shots, shots), steps * shots)
            total[...] += dot(rows[window, :], blocks[slot, k])
            return carry

        lax.fori_loop(first, last, add, None)
        if slot < NEAR - 1:
            messages[slot][...] = total[:shots, :].astype(jnp.bfloat16)
        else:
            own[...] = total[:shots, :]
        for s in range(1, steps):
            rest[s - 1][slot * shots : (slot + 1) * shots, :] = total[
                s * shots : (s + 1) * shots, :
            ].astype(jnp.bfloat16)


def step_kernel(step, last_step, ranges, source, inverse, own, *refs):
    shots, tile_len = own.shape
    refs = list(refs)
    received = [refs.pop(0) for _ in range(1 if step == 0 else NEAR - 1)]
    right = source[step * shots : (step + 1) * shots, :] - own[...]
    for block in received:
        right = right - block[...].astype(jnp.float32)
    if last_step:
        (natural,) = refs
        density = dot(right.astype(jnp.bfloat16), inverse[...])
        natural[...] = density.T.astype(jnp.bfloat16)
        return
    weights, rest, rest_far = refs[:3]
    refs = refs[3:]
    olders, refs = refs[:step], refs[step:]
    natural, density_ref, next_own = refs[:3]
    messages = refs[3:]
    density = dot(right.astype(jnp.bfloat16), inverse[...])
    rounded = density.astype(jnp.bfloat16)
    density_ref[...] = rounded
    band_zero = lax.axis_index("lag") == 0
    recent = [rounded] + [ref[...] for ref in olders]
    for slot, offset in enumerate(slot_offsets(lax.axis_index("patch"))):
        part = slice(slot * shots, (slot + 1) * shots)
        terms = rest[part, :].astype(jnp.float32) + rest_far[part, :].astype(jnp.float32)
        columns = pl.ds(pl.multiple_of(offset * tile_len, tile_len), tile_len)
        for k, block in enumerate(recent):
            lag = k + 1
            live = band_zero & (ranges[0, offset] <= lag) & (lag < ranges[0, NEAR + offset])
            scale = jnp.where(live, 1.0, 0.0).astype(jnp.float32)
            terms = terms + scale * dot(block, weights[k, :, columns])
        if slot < NEAR - 1:
            messages[slot][...] = terms.astype(jnp.bfloat16)
        else:
            next_own[...] = terms
    natural[...] = density.T.astype(jnp.bfloat16)


def call(kernel, outs, specs, scratch=(), name=None):
    shapes = [jax.ShapeDtypeStruct(shape, dtype) for shape, dtype in outs]
    return pl.pallas_call(
        kernel,
        out_shape=shapes,
        in_specs=[pl.BlockSpec(memory_space=space) for space in specs],
        out_specs=[pl.BlockSpec(memory_space=VMEM)] * len(shapes),
        scratch_shapes=list(scratch),
        name=name,
    )


def lag_partners(lags, distance):
    return [(i, i ^ distance) for i in range(lags)]


def lag_sum(block, lags):
    far, distance = None, 1
    while distance < lags:
        if far is not None:
            block = block + far.astype(block.dtype)
        far = lax.ppermute(block.astype(jnp.bfloat16), "lag", lag_partners(lags, distance))
        distance *= 2
    return block, far


def from_band_zero(block, lags):
    index = lax.axis_index("lag")
    distance = 1
    while distance < lags:
        far = lax.ppermute(block, "lag", lag_partners(lags, distance))
        block = jnp.where(index < distance, block, far)
        distance *= 2
    return block


def local(interaction, history, near_inverse, lag_ranges, receiver_tile, receiver_panel, residuals):
    tile_len = near_inverse.shape[1]
    band, _, shots = history.shape
    recv, steps, _ = residuals.shape
    patches, lags = lax.axis_size("patch"), lax.axis_size("lag")
    width = steps * shots
    f32, bf16 = jnp.float32, jnp.bfloat16
    block = (shots, tile_len)
    routes = pairings(patches)

    rim = lax.ppermute(
        history[band - steps + 1 :], "lag", [(i, (i + 1) % lags) for i in range(lags)]
    )
    (outgoing,) = call(
        pack_kernel, [((patches * CAP, width + LANES), bf16)], [VMEM] * 3, name="pack"
    )(receiver_tile.reshape(1, recv), receiver_panel.reshape(1, recv), residuals.reshape(recv, width))
    arrived = lax.all_to_all(
        outgoing.reshape(patches, CAP, width + LANES), "patch", split_axis=0, concat_axis=0, tiled=True
    ).reshape(patches * CAP, width + LANES)
    (source,) = call(source_kernel, [((width, tile_len), f32)], [VMEM], name="source")(arrived)

    older = call(
        functools.partial(older_kernel, steps),
        [(block, bf16)] * (NEAR - 1) + [(block, f32)] + [((NEAR * shots, tile_len), bf16)] * (steps - 1),
        [pltpu.SMEM, VMEM, VMEM, pl.ANY],
        [
            VMEM(((band + steps - 1) * shots, tile_len), bf16),
            VMEM((NEAR, band, tile_len, tile_len), bf16),
            VMEM((width, tile_len), f32),
            pltpu.SemaphoreType.DMA((NEAR, band)),
        ],
        name="older",
    )(lag_ranges, rim, history, interaction)
    messages, own, rest = older[: NEAR - 1], older[NEAR - 1], older[NEAR:]

    def exchange(blocks):
        return [lax.ppermute(b, "patch", r) for b, r in zip(blocks, routes)]

    for incoming in exchange(messages):
        own = own + incoming.astype(f32)
    own, far = lag_sum(own, lags)
    received = [far]
    pairs = [lag_sum(r, lags) for r in rest]

    recent_weights = interaction[: steps - 1]
    densities, naturals = [], []
    for step in range(steps):
        last_step = step == steps - 1
        inputs = [lag_ranges, source, near_inverse, own, *received]
        outs = [((tile_len, shots), bf16)]
        if not last_step:
            inputs += [recent_weights, *pairs[step], *densities[::-1]]
            outs += [(block, bf16), (block, f32)] + [(block, bf16)] * (NEAR - 1)
        results = call(
            functools.partial(step_kernel, step, last_step),
            outs,
            [pltpu.SMEM] + [VMEM] * (len(inputs) - 1),
            name=f"step{step}",
        )(*inputs)
        naturals.append(results[0])
        if not last_step:
            densities.append(results[1])
            own = results[2]
            received = exchange(results[3:])
    early = from_band_zero(jnp.stack(naturals[:-1]), lags)
    late = from_band_zero(naturals[-1], lags)
    return jnp.concatenate([early, late[None]], 0)


def solution(mesh):
    in_specs = (
        P("lag", "patch", None),
        P("lag", "patch", None),
        P("patch", None),
        P("patch", None),
        P("patch", None),
        P("patch"),
        P("patch", None, None),
    )
    out_specs = P(None, "patch", None)
    return jax.shard_map(local, mesh=mesh, in_specs=in_specs, out_specs=out_specs, check_vma=False)
```

```python
import functools

import jax
import jax.numpy as jnp
from jax import lax
from jax.experimental import pallas as pl
from jax.experimental.pallas import tpu as pltpu
from jax.sharding import PartitionSpec as P

NEAR = 5
CAP = 16
HALF = NEAR // 2
LANES = 128
VMEM = pltpu.VMEM


def dot(left, right):
    return jnp.dot(left, right, preferred_element_type=jnp.float32)


def slot_offsets(patch):
    odd = lax.rem(patch, 2)
    high = lax.rem(lax.div(patch, 2), 2)
    return [4 * high, 1 + 2 * odd, 4 - 4 * high, 3 - 2 * odd, HALF]


def pairings(patches):
    far = [(i + 2 if i & 2 else i - 2) % patches for i in range(patches)]
    odd_even = [(i + 1 if i & 1 else i - 1) % patches for i in range(patches)]
    near = [i ^ 2 for i in range(patches)]
    core = [i ^ 1 for i in range(patches)]
    return [list(enumerate(p)) for p in (far, odd_even, near, core)]


def pack_kernel(tile_ref, panel_ref, rows_ref, out_ref):
    recv = rows_ref.shape[0]
    width = rows_ref.shape[1]
    slots = out_ref.shape[0]
    patches = slots // CAP
    tile = tile_ref[...]
    hot = lax.broadcasted_iota(jnp.int32, (patches, recv), 0) == tile
    before = lax.broadcasted_iota(jnp.int32, (recv, recv), 0) < lax.broadcasted_iota(
        jnp.int32, (recv, recv), 1
    )
    hot = jnp.where(hot, 1.0, 0.0)
    ahead = dot(hot.astype(jnp.bfloat16), jnp.where(before, 1.0, 0.0).astype(jnp.bfloat16))
    earlier = jnp.sum(hot * ahead, axis=0, keepdims=True).astype(jnp.int32)
    slot = tile * CAP + earlier
    placed = lax.broadcasted_iota(jnp.int32, (slots, recv), 0) == slot
    placer = jnp.where(placed, 1.0, 0.0).astype(jnp.bfloat16)
    out_ref[:, :width] = dot(placer, rows_ref[...]).astype(jnp.bfloat16)
    marks = jnp.where(placed, (panel_ref[...] + 1).astype(jnp.float32), 0.0)
    label = jnp.sum(marks, axis=1, keepdims=True)
    out_ref[:, width:] = jnp.broadcast_to(label, (slots, LANES)).astype(jnp.bfloat16)


def source_kernel(arrived_ref, *outs):
    slots = arrived_ref.shape[0]
    shots, tile_len = outs[0].shape
    width = len(outs) * shots
    label = arrived_ref[:, width:].astype(jnp.float32)
    lane = lax.broadcasted_iota(jnp.int32, (slots, LANES), 1)
    picker = jnp.concatenate(
        [
            jnp.where(label == (lane + (1 + first)).astype(jnp.float32), 1.0, 0.0)
            for first in range(0, tile_len, LANES)
        ],
        axis=1,
    ).astype(jnp.bfloat16)
    for step, out in enumerate(outs):
        out[...] = lax.dot_general(
            arrived_ref[:, step * shots : (step + 1) * shots],
            picker,
            (((0,), (0,)), ((), ())),
            preferred_element_type=jnp.float32,
        )


def older_kernel(steps, sizes, ranges, rim, history, inverse_hbm, weights, *refs):
    outs, (rows, blocks, sems, out_sems) = refs[:-4], refs[-4:]
    messages, outs = outs[: NEAR - 1], outs[NEAR - 1 :]
    own, stage, recent, inverse = outs[:4]
    rest = outs[4:]
    band, tile_len, shots = history.shape
    lag = lax.axis_index("lag")
    offsets = slot_offsets(lax.axis_index("patch"))

    def bounds(offset):
        base = lag * band + 1
        first = jnp.clip(ranges[0, offset] - base, 0, band)
        last = jnp.clip(ranges[0, NEAR + offset] - base, 0, band)
        return first, last

    def fetch(slot, offset, k):
        columns = pl.ds(pl.multiple_of(offset * tile_len, tile_len), tile_len)
        return pltpu.make_async_copy(
            weights.at[k, :, columns], blocks.at[slot, k], sems.at[slot, k]
        )

    def send(slot, step, target):
        return pltpu.make_async_copy(
            stage.at[slot, pl.ds(step * shots, shots)], target, out_sems.at[slot, step]
        )

    for slot, offset in enumerate(offsets):
        first, last = bounds(offset)
        lax.fori_loop(first, last, lambda k, c, s=slot, o=offset: fetch(s, o, k).start(), None)
    keep = [
        pltpu.make_async_copy(weights.at[pl.ds(0, steps - 1)], recent, out_sems.at[NEAR, 0]),
        pltpu.make_async_copy(inverse_hbm, inverse, out_sems.at[NEAR, 1]),
    ]
    for copy in keep:
        copy.start()
    for k in range(band):
        rows[(band - 1 - k) * shots : (band - k) * shots, :] = history[k].T

    @pl.when(lag > 0)
    def _():
        for k in range(steps - 1):
            at = (band + steps - 2 - k) * shots
            rows[at : at + shots, :] = rim[k].T

    @pl.when(lag == 0)
    def _():
        rows[band * shots :, :] = jnp.zeros(((steps - 1) * shots, tile_len), jnp.bfloat16)

    def window(k):
        return rows[pl.ds(pl.multiple_of((band - 1 - k) * shots, shots), steps * shots), :]

    def one_slot(slot, carry):
        offset = offsets[-1]
        for j in range(NEAR - 1):
            offset = jnp.where(slot == j, offsets[j], offset)
        first, last = bounds(offset)
        lax.fori_loop(first, last, lambda k, c: fetch(slot, offset, k).wait(), None)

        def emit(total):
            stage[slot] = total.astype(jnp.bfloat16)

            @pl.when(slot == NEAR - 1)
            def _():
                own[...] = total[:shots]

        def branch(size):
            def run():
                start = jnp.minimum(first, band - size)
                left, right = [], []
                for i in range(size):
                    k = start + i
                    live = (k >= first) & (k < last)
                    tile = blocks[slot, k]
                    left.append(window(k))
                    right.append(jnp.where(live, tile, jnp.zeros_like(tile)))
                emit(dot(jnp.concatenate(left, axis=1), jnp.concatenate(right, axis=0)))

            return run

        count = last - first
        which = jnp.where(count > 0, 1, 0)
        for i, size in enumerate(sizes[:-1]):
            which = jnp.where(count > size, i + 2, which)
        lax.switch(
            which,
            [lambda: emit(jnp.zeros((steps * shots, tile_len), jnp.float32))]
            + [branch(size) for size in sizes],
        )
        for j in range(NEAR - 1):
            pl.when(slot == j)(lambda j=j: send(j, 0, messages[j]).start())
        for step in range(1, steps):
            send(slot, step, rest[step - 1].at[pl.ds(slot * shots, shots)]).start()
        return carry

    lax.fori_loop(0, NEAR, one_slot, None)
    for copy in keep:
        copy.wait()
    for slot in range(NEAR):
        if slot < NEAR - 1:
            send(slot, 0, messages[slot]).wait()
        for step in range(1, steps):
            send(slot, step, rest[step - 1].at[pl.ds(slot * shots, shots)]).wait()


def step_kernel(step, last_step, ranges, source, inverse, own, *refs):
    shots = own.shape[0]
    tile_len = own.shape[1]
    refs = list(refs)
    received = [refs.pop(0) for _ in range(1 if step == 0 else NEAR - 1)]
    right = source[...] - own[...]
    for block in received:
        right = right - block[...].astype(jnp.float32)
    density = dot(right.astype(jnp.bfloat16), inverse[...])
    if last_step:
        (natural,) = refs
        natural[...] = density.T.astype(jnp.bfloat16)
        return
    weights, stage, rest_far = refs[:3]
    olders, outs = refs[3 : 3 + step], refs[3 + step :]
    density_ref, next_own = outs[:2]
    messages = outs[2:]
    rounded = density.astype(jnp.bfloat16)
    density_ref[...] = rounded
    band_zero = lax.axis_index("lag") == 0
    recent = [rounded] + [ref[...] for ref in olders]
    nxt = step + 1
    for slot, offset in enumerate(slot_offsets(lax.axis_index("patch"))):
        terms = stage[slot, nxt * shots : (nxt + 1) * shots, :].astype(jnp.float32)
        terms = terms + rest_far[slot * shots : (slot + 1) * shots, :].astype(jnp.float32)
        columns = pl.ds(pl.multiple_of(offset * tile_len, tile_len), tile_len)
        for k, block in enumerate(recent):
            lag = k + 1
            live = band_zero & (ranges[0, offset] <= lag) & (lag < ranges[0, NEAR + offset])
            scale = jnp.where(live, 1.0, 0.0).astype(jnp.float32)
            terms = terms + scale * dot(block, weights[k, :, columns])
        if slot < NEAR - 1:
            messages[slot][...] = terms.astype(jnp.bfloat16)
        else:
            next_own[...] = terms


def natural_kernel(*refs):
    blocks, out = refs[:-1], refs[-1]
    for k, block in enumerate(blocks):
        out[k] = block[...].astype(jnp.float32).T.astype(jnp.bfloat16)


def early_kernel(near_lags, mine, far, out, sem):
    def move(block):
        copy = pltpu.make_async_copy(block, out.at[pl.ds(0, block.shape[0])], sem)
        copy.start()
        copy.wait()

    keeps = lax.axis_index("lag") < near_lags
    pl.when(keeps)(lambda: move(mine))
    pl.when(jnp.logical_not(keeps))(lambda: move(far))


def late_kernel(near_lags, begun, mine, far, out, sem):
    del begun

    def move(block):
        copy = pltpu.make_async_copy(block, out.at[out.shape[0] - 1], sem)
        copy.start()
        copy.wait()

    keeps = lax.axis_index("lag") < near_lags
    pl.when(keeps)(lambda: move(mine))
    pl.when(jnp.logical_not(keeps))(lambda: move(far))


def call(kernel, outs, specs, scratch=(), out_specs=None, aliases=None, limit=8 << 20):
    made = []
    for shape, dtype, *space in outs:
        made.append(space[0](shape, dtype) if space else jax.ShapeDtypeStruct(shape, dtype))
    return pl.pallas_call(
        kernel,
        out_shape=made,
        in_specs=[pl.BlockSpec(memory_space=space) for space in specs],
        out_specs=[pl.BlockSpec(memory_space=s) for s in (out_specs or [VMEM] * len(made))],
        scratch_shapes=list(scratch),
        input_output_aliases=aliases or {},
        compiler_params=pltpu.CompilerParams(vmem_limit_bytes=limit),
    )


def near_memory(array):
    return pltpu.with_memory_space_constraint(array, VMEM)


def lag_partners(lags, distance):
    return [(i, i ^ distance) for i in range(lags)]


def lag_sum(block, lags):
    far, distance = None, 1
    while distance < lags:
        if far is not None:
            block = block + far.astype(block.dtype)
        far = lax.ppermute(block.astype(jnp.bfloat16), "lag", lag_partners(lags, distance))
        distance *= 2
    return block, far


def from_band_zero(block, lags):
    index = lax.axis_index("lag")
    distance = 1
    far = block
    while distance < lags:
        if distance > 1:
            block = jnp.where(index < distance // 2, block, far)
        far = lax.ppermute(block, "lag", lag_partners(lags, distance))
        distance *= 2
    return block, far


def local(interaction, history, near_inverse, lag_ranges, receiver_tile, receiver_panel, residuals):
    tile_len = near_inverse.shape[1]
    band, _, shots = history.shape
    recv, steps, _ = residuals.shape
    patches, lags = lax.axis_size("patch"), lax.axis_size("lag")
    width = steps * shots
    f32, bf16 = jnp.float32, jnp.bfloat16
    block = (shots, tile_len)
    routes = pairings(patches)

    rim = lax.ppermute(
        history[band - steps + 1 :], "lag", [(i, (i + 1) % lags) for i in range(lags)]
    )
    (outgoing,) = call(
        pack_kernel, [((patches * CAP, width + LANES), bf16)], [VMEM] * 3
    )(receiver_tile.reshape(1, recv), receiver_panel.reshape(1, recv), residuals.reshape(recv, width))
    arrived = lax.all_to_all(
        outgoing.reshape(patches, CAP, width + LANES),
        "patch",
        split_axis=0,
        concat_axis=0,
        tiled=True,
    ).reshape(patches * CAP, width + LANES)
    source = call(source_kernel, [(block, f32, VMEM)] * steps, [VMEM])(arrived)
    source = [near_memory(s) for s in source]

    sizes = sorted({-(-band // 4), -(-band // 2), band})
    older = call(
        functools.partial(older_kernel, steps, sizes),
        [(block, bf16)] * (NEAR - 1)
        + [
            (block, f32, VMEM),
            ((NEAR, width, tile_len), bf16, VMEM),
            ((steps - 1, tile_len, NEAR * tile_len), bf16, VMEM),
            ((tile_len, tile_len), bf16, VMEM),
        ]
        + [((NEAR * shots, tile_len), bf16)] * (steps - 1),
        [pltpu.SMEM, VMEM, VMEM, pltpu.HBM, pltpu.HBM],
        [
            VMEM(((band + steps - 1) * shots, tile_len), bf16),
            VMEM((NEAR, band, tile_len, tile_len), bf16),
            pltpu.SemaphoreType.DMA((NEAR, band)),
            pltpu.SemaphoreType.DMA((NEAR + 1, steps)),
        ],
        out_specs=[pl.ANY] * (NEAR - 1) + [VMEM] * 4 + [pl.ANY] * (steps - 1),
        limit=54 << 20,
    )(lag_ranges, rim, history, near_inverse, interaction)
    messages, (own, stage, recent, inverse), rest = older[: NEAR - 1], older[NEAR - 1 : NEAR + 3], older[NEAR + 3 :]
    stage, recent, inverse = near_memory(stage), near_memory(recent), near_memory(inverse)

    def exchange(blocks):
        gone = []
        for b, r in zip(blocks, routes):
            gone.append(lax.ppermute(b, "patch", r))
        return gone

    for incoming in exchange(messages):
        own = own + incoming.astype(f32)
    own, far = lag_sum(own, lags)
    received = [far]
    pairs = []
    for r in rest:
        pairs.append(lag_sum(r, lags))

    densities = []
    for step in range(steps):
        last_step = step == steps - 1
        inputs = [lag_ranges, source[step], inverse, own, *received]
        if last_step:
            outs = [((tile_len, shots), bf16)]
        else:
            here, there = pairs[step]
            if lags > 2:
                there = there + (here - rest[step])
            inputs += [recent, stage, there, *densities[::-1]]
            outs = [(block, bf16, VMEM), (block, f32, VMEM)] + [(block, bf16)] * (NEAR - 1)
        results = call(
            functools.partial(step_kernel, step, last_step),
            outs,
            [pltpu.SMEM] + [VMEM] * (len(inputs) - 1),
        )(*inputs)
        if not last_step:
            densities.append(near_memory(results[0]))
            own = near_memory(results[1])
            received = exchange(results[2:])
    (early,) = call(
        natural_kernel, [((steps - 1, tile_len, shots), bf16)], [VMEM] * (steps - 1)
    )(*densities)
    early = from_band_zero(early, lags)
    late = from_band_zero(results[0], lags)
    whole = ((steps, tile_len, shots), bf16)
    (begun,) = call(
        functools.partial(early_kernel, lags // 2),
        [whole],
        [pl.ANY] * 2,
        [pltpu.SemaphoreType.DMA],
        out_specs=[pl.ANY],
    )(*early)
    (out,) = call(
        functools.partial(late_kernel, lags // 2),
        [whole],
        [pl.ANY] * 3,
        [pltpu.SemaphoreType.DMA],
        out_specs=[pl.ANY],
        aliases={0: 0},
    )(begun, *late)
    return out


def solution(mesh):
    in_specs = (
        P("lag", "patch", None),
        P("lag", "patch", None),
        P("patch", None),
        P("patch", None),
        P("patch", None),
        P("patch"),
        P("patch", None, None),
    )
    out_specs = P(None, "patch", None)

    return jax.shard_map(local, mesh=mesh, in_specs=in_specs, out_specs=out_specs, check_vma=False)
```

```python
import functools

import jax
import jax.numpy as jnp
from jax import lax
from jax.experimental import pallas as pl
from jax.experimental.pallas import tpu as pltpu
from jax.sharding import PartitionSpec as P

NEAR = 5
CAP = 16
HALF = NEAR // 2
LANES = 128
VMEM = pltpu.VMEM
PREPARE_LIMIT = 97 << 19
OLDER_LIMIT = 97 << 19


def dot(left, right):
    return jnp.dot(left, right, preferred_element_type=jnp.float32)


def slot_offsets(patch):
    odd = lax.rem(patch, 2)
    high = lax.rem(lax.div(patch, 2), 2)
    return [4 * high, 1 + 2 * odd, 4 - 4 * high, 3 - 2 * odd, HALF]


def pairings(patches):
    far = [(i + 2 if i & 2 else i - 2) % patches for i in range(patches)]
    odd_even = [(i + 1 if i & 1 else i - 1) % patches for i in range(patches)]
    near = [i ^ 2 for i in range(patches)]
    core = [i ^ 1 for i in range(patches)]
    return [list(enumerate(p)) for p in (far, odd_even, near, core)]


def active(ranges, offset, lag, band):
    base = lag * band + 1
    first = jnp.clip(ranges[0, offset] - base, 0, band)
    last = jnp.clip(ranges[0, NEAR + offset] - base, 0, band)
    return first, last


def pack(tile_ref, panel_ref, rows_ref, out_ref):
    recv = rows_ref.shape[0]
    slots, width = out_ref.shape
    width = width - LANES
    patches = slots // CAP
    tile = tile_ref[...]
    hot = lax.broadcasted_iota(jnp.int32, (patches, recv), 0) == tile
    before = lax.broadcasted_iota(jnp.int32, (recv, recv), 0) < lax.broadcasted_iota(
        jnp.int32, (recv, recv), 1
    )
    hot = jnp.where(hot, 1.0, 0.0)
    ahead = dot(hot.astype(jnp.bfloat16), jnp.where(before, 1.0, 0.0).astype(jnp.bfloat16))
    earlier = jnp.sum(hot * ahead, axis=0, keepdims=True).astype(jnp.int32)
    slot = tile * CAP + earlier
    placed = lax.broadcasted_iota(jnp.int32, (slots, recv), 0) == slot
    placer = jnp.where(placed, 1.0, 0.0).astype(jnp.bfloat16)
    piece = lax.rem(lax.axis_index("lag"), rows_ref.shape[1] // width)
    rows = rows_ref[:, pl.ds(pl.multiple_of(piece * width, width), width)]
    out_ref[:, :width] = dot(placer, rows).astype(jnp.bfloat16)
    marks = jnp.where(placed, (panel_ref[...] + 1).astype(jnp.float32), 0.0)
    label = jnp.sum(marks, axis=1, keepdims=True)
    out_ref[:, width:] = jnp.broadcast_to(label, (slots, LANES)).astype(jnp.bfloat16)


def prepare_kernel(ranges, tile, panel, residuals, history, inverse, weights, *refs):
    outgoing, blocks, near_history, recent, near_inverse, sems, keep_sems = refs
    _, band, tile_len, _ = blocks.shape
    lag = lax.axis_index("lag")

    def fetch(slot, offset, k):
        columns = pl.ds(pl.multiple_of(offset * tile_len, tile_len), tile_len)
        return pltpu.make_async_copy(
            weights.at[k, :, columns], blocks.at[slot, k], sems.at[slot, k]
        )

    offsets = slot_offsets(lax.axis_index("patch"))
    for slot, offset in enumerate(offsets):
        first, last = active(ranges, offset, lag, band)
        lax.fori_loop(first, last, lambda k, c, s=slot, o=offset: fetch(s, o, k).start(), None)
    keep = [
        pltpu.make_async_copy(history, near_history, keep_sems.at[0]),
        pltpu.make_async_copy(weights.at[pl.ds(0, recent.shape[0])], recent, keep_sems.at[1]),
        pltpu.make_async_copy(inverse, near_inverse, keep_sems.at[2]),
    ]
    for copy in keep:
        copy.start()
    pack(tile, panel, residuals, outgoing)
    for copy in keep:
        copy.wait()
    for slot, offset in enumerate(offsets):
        first, last = active(ranges, offset, lag, band)
        lax.fori_loop(first, last, lambda k, c, s=slot, o=offset: fetch(s, o, k).wait(), None)


def source_kernel(shots, arrived_ref, out):
    slots = arrived_ref.shape[0]
    width, tile_len = out.shape
    label = arrived_ref[:, width:].astype(jnp.float32)
    lane = lax.broadcasted_iota(jnp.int32, (slots, LANES), 1)
    picker = jnp.concatenate(
        [
            jnp.where(label == (lane + (1 + first)).astype(jnp.float32), 1.0, 0.0)
            for first in range(0, tile_len, LANES)
        ],
        axis=1,
    ).astype(jnp.bfloat16)
    for first in range(0, width, shots):
        out[first : first + shots, :] = lax.dot_general(
            arrived_ref[:, first : first + shots],
            picker,
            (((0,), (0,)), ((), ())),
            preferred_element_type=jnp.float32,
        )


def older_kernel(steps, sizes, ranges, rim, history, blocks, *refs):
    outs, (rows, out_sems) = refs[:-2], refs[-2:]
    messages, outs = outs[: NEAR - 1], outs[NEAR - 1 :]
    own, stage = outs[:2]
    rest = outs[2:]
    band, tile_len, shots = history.shape
    lag = lax.axis_index("lag")
    offsets = slot_offsets(lax.axis_index("patch"))

    def send(slot, step, target):
        return pltpu.make_async_copy(
            stage.at[slot, pl.ds(step * shots, shots)], target, out_sems.at[slot, step]
        )

    for k in range(band):
        rows[(band - 1 - k) * shots : (band - k) * shots, :] = history[k].T

    @pl.when(lag > 0)
    def _():
        for k in range(steps - 1):
            at = (band + steps - 2 - k) * shots
            rows[at : at + shots, :] = rim[k].T

    @pl.when(lag == 0)
    def _():
        rows[band * shots :, :] = jnp.zeros(((steps - 1) * shots, tile_len), jnp.bfloat16)

    def window(k):
        return rows[pl.ds(pl.multiple_of((band - 1 - k) * shots, shots), steps * shots), :]

    def one_slot(slot, carry):
        offset = offsets[-1]
        for j in range(NEAR - 1):
            offset = jnp.where(slot == j, offsets[j], offset)
        first, last = active(ranges, offset, lag, band)

        def emit(total):
            stage[slot] = total.astype(jnp.bfloat16)

            @pl.when(slot == NEAR - 1)
            def _():
                own[...] = total[:shots]

        def branch(size):
            def run():
                start = jnp.minimum(first, band - size)
                left, right = [], []
                for i in range(size):
                    k = start + i
                    live = (k >= first) & (k < last)
                    tile = blocks[slot, k]
                    left.append(window(k))
                    right.append(jnp.where(live, tile, jnp.zeros_like(tile)))
                emit(dot(jnp.concatenate(left, axis=1), jnp.concatenate(right, axis=0)))

            return run

        count = last - first
        which = jnp.where(count > 0, 1, 0)
        for i, size in enumerate(sizes[:-1]):
            which = jnp.where(count > size, i + 2, which)
        lax.switch(
            which,
            [lambda: emit(jnp.zeros((steps * shots, tile_len), jnp.float32))]
            + [branch(size) for size in sizes],
        )
        for j in range(NEAR - 1):
            pl.when(slot == j)(lambda j=j: send(j, 0, messages[j]).start())
        for step in range(1, steps):
            send(slot, step, rest[step - 1].at[pl.ds(slot * shots, shots)]).start()
        return carry

    lax.fori_loop(0, NEAR, one_slot, None)
    for slot in range(NEAR):
        if slot < NEAR - 1:
            send(slot, 0, messages[slot]).wait()
        for step in range(1, steps):
            send(slot, step, rest[step - 1].at[pl.ds(slot * shots, shots)]).wait()


def step_kernel(step, last_step, ranges, source, inverse, own, *refs):
    shots = own.shape[0]
    tile_len = own.shape[1]
    refs = list(refs)
    received = [refs.pop(0) for _ in range(1 if step == 0 else NEAR - 1)]
    at = step % (source.shape[0] // shots) * shots
    right = source[at : at + shots, :] - own[...]
    for block in received:
        right = right - block[...].astype(jnp.float32)
    density = dot(right.astype(jnp.bfloat16), inverse[...])
    if last_step:
        (natural,) = refs
        natural[...] = density.T.astype(jnp.bfloat16)
        return
    weights, stage, rest_far = refs[:3]
    olders, outs = refs[3 : 3 + step], refs[3 + step :]
    density_ref, next_own = outs[:2]
    messages = outs[2:]
    rounded = density.astype(jnp.bfloat16)
    density_ref[...] = rounded
    band_zero = lax.axis_index("lag") == 0
    recent = [rounded] + [ref[...] for ref in olders]
    nxt = step + 1
    for slot, offset in enumerate(slot_offsets(lax.axis_index("patch"))):
        terms = stage[slot, nxt * shots : (nxt + 1) * shots, :].astype(jnp.float32)
        terms = terms + rest_far[slot * shots : (slot + 1) * shots, :].astype(jnp.float32)
        columns = pl.ds(pl.multiple_of(offset * tile_len, tile_len), tile_len)
        for k, block in enumerate(recent):
            lag = k + 1
            live = band_zero & (ranges[0, offset] <= lag) & (lag < ranges[0, NEAR + offset])
            scale = jnp.where(live, 1.0, 0.0).astype(jnp.float32)
            terms = terms + scale * dot(block, weights[k, :, columns])
        if slot < NEAR - 1:
            messages[slot][...] = terms.astype(jnp.bfloat16)
        else:
            next_own[...] = terms


def natural_kernel(*refs):
    blocks, out = refs[:-1], refs[-1]
    for k, block in enumerate(blocks):
        out[k] = block[...].astype(jnp.float32).T.astype(jnp.bfloat16)


def early_kernel(near_lags, mine, far, out, sem):
    def move(block):
        copy = pltpu.make_async_copy(block, out.at[pl.ds(0, block.shape[0])], sem)
        copy.start()
        copy.wait()

    keeps = lax.axis_index("lag") < near_lags
    pl.when(keeps)(lambda: move(mine))
    pl.when(jnp.logical_not(keeps))(lambda: move(far))


def late_kernel(near_lags, begun, mine, far, out, sem):
    del begun

    def move(block):
        copy = pltpu.make_async_copy(block, out.at[out.shape[0] - 1], sem)
        copy.start()
        copy.wait()

    keeps = lax.axis_index("lag") < near_lags
    pl.when(keeps)(lambda: move(mine))
    pl.when(jnp.logical_not(keeps))(lambda: move(far))


def call(kernel, outs, specs, scratch=(), out_specs=None, aliases=None, limit=8 << 20):
    made = []
    for shape, dtype, *space in outs:
        made.append(space[0](shape, dtype) if space else jax.ShapeDtypeStruct(shape, dtype))
    return pl.pallas_call(
        kernel,
        out_shape=made,
        in_specs=[pl.BlockSpec(memory_space=space) for space in specs],
        out_specs=[pl.BlockSpec(memory_space=s) for s in (out_specs or [VMEM] * len(made))],
        scratch_shapes=list(scratch),
        input_output_aliases=aliases or {},
        compiler_params=pltpu.CompilerParams(vmem_limit_bytes=limit),
    )


def near_memory(array):
    return pltpu.with_memory_space_constraint(array, VMEM)


def lag_partners(lags, distance):
    return [(i, i ^ distance) for i in range(lags)]


def lag_sum(block, lags):
    far, distance = None, 1
    while distance < lags:
        if far is not None:
            block = block + far.astype(block.dtype)
        far = lax.ppermute(block.astype(jnp.bfloat16), "lag", lag_partners(lags, distance))
        distance *= 2
    return block, far


def from_band_zero(block, lags):
    index = lax.axis_index("lag")
    distance = 1
    far = block
    while distance < lags:
        if distance > 1:
            block = jnp.where(index < distance // 2, block, far)
        far = lax.ppermute(block, "lag", lag_partners(lags, distance))
        distance *= 2
    return block, far


def local(interaction, history, near_inverse, lag_ranges, receiver_tile, receiver_panel, residuals):
    tile_len = near_inverse.shape[1]
    band, _, shots = history.shape
    recv, steps, _ = residuals.shape
    patches, lags = lax.axis_size("patch"), lax.axis_size("lag")
    width = steps * shots
    f32, bf16 = jnp.float32, jnp.bfloat16
    block = (shots, tile_len)
    routes = pairings(patches)

    rim = lax.ppermute(
        history[band - steps + 1 :], "lag", [(i, (i + 1) % lags) for i in range(lags)]
    )
    pieces = min(lags, steps)
    piece = width // pieces
    outgoing, blocks, near_history, recent, inverse = call(
        prepare_kernel,
        [
            ((patches * CAP, piece + LANES), bf16),
            ((NEAR, band, tile_len, tile_len), bf16, VMEM),
            ((band, tile_len, shots), bf16, VMEM),
            ((steps - 1, tile_len, NEAR * tile_len), bf16, VMEM),
            ((tile_len, tile_len), bf16, VMEM),
        ],
        [pltpu.SMEM] + [VMEM] * 3 + [pltpu.HBM] * 3,
        [pltpu.SemaphoreType.DMA((NEAR, band)), pltpu.SemaphoreType.DMA((3,))],
        limit=PREPARE_LIMIT,
    )(
        lag_ranges,
        receiver_tile.reshape(1, recv),
        receiver_panel.reshape(1, recv),
        residuals.reshape(recv, width),
        history,
        near_inverse,
        interaction,
    )
    blocks, near_history = near_memory(blocks), near_memory(near_history)
    recent, inverse = near_memory(recent), near_memory(inverse)

    sizes = sorted({-(-band // 4), -(-band // 2), band})
    older = call(
        functools.partial(older_kernel, steps, sizes),
        [(block, bf16)] * (NEAR - 1)
        + [(block, f32), ((NEAR, width, tile_len), bf16, VMEM)]
        + [((NEAR * shots, tile_len), bf16)] * (steps - 1),
        [pltpu.SMEM] + [VMEM] * 3,
        [
            VMEM(((band + steps - 1) * shots, tile_len), bf16),
            pltpu.SemaphoreType.DMA((NEAR, steps)),
        ],
        out_specs=[pl.ANY] * (NEAR - 1) + [VMEM] * 2 + [pl.ANY] * (steps - 1),
        limit=OLDER_LIMIT,
    )(lag_ranges, rim, near_history, blocks)
    messages, (own, stage), rest = older[: NEAR - 1], older[NEAR - 1 : NEAR + 1], older[NEAR + 1 :]
    stage = near_memory(stage)

    arrived = lax.all_to_all(
        outgoing.reshape(patches, CAP, piece + LANES),
        "patch",
        split_axis=0,
        concat_axis=0,
        tiled=True,
    ).reshape(patches * CAP, piece + LANES)
    (mine,) = call(
        functools.partial(source_kernel, shots), [((piece, tile_len), f32)], [VMEM]
    )(arrived)
    source = [mine]
    for k in range(1, pieces):
        source.append(lax.ppermute(mine, "lag", [(i, (i - k) % lags) for i in range(lags)]))

    def exchange(blocks):
        gone = []
        for b, r in zip(blocks, routes):
            gone.append(lax.ppermute(b, "patch", r))
        return gone

    for incoming in exchange(messages):
        own = own + incoming.astype(f32)
    own, far = lag_sum(own, lags)
    received = [far]
    pairs = []
    for r in rest:
        pairs.append(lag_sum(r, lags))

    densities = []
    for step in range(steps):
        last_step = step == steps - 1
        inputs = [lag_ranges, source[step * pieces // steps], inverse, own, *received]
        if last_step:
            outs = [((tile_len, shots), bf16)]
        else:
            here, there = pairs[step]
            if lags > 2:
                there = there + (here - rest[step])
            inputs += [recent, stage, there, *densities[::-1]]
            outs = [(block, bf16, VMEM), (block, f32, VMEM)] + [(block, bf16)] * (NEAR - 1)
        results = call(
            functools.partial(step_kernel, step, last_step),
            outs,
            [pltpu.SMEM] + [VMEM] * (len(inputs) - 1),
        )(*inputs)
        if not last_step:
            densities.append(near_memory(results[0]))
            own = near_memory(results[1])
            received = exchange(results[2:])
    (early,) = call(
        natural_kernel, [((steps - 1, tile_len, shots), bf16)], [VMEM] * (steps - 1)
    )(*densities)
    early = from_band_zero(early, lags)
    late = from_band_zero(results[0], lags)
    whole = ((steps, tile_len, shots), bf16)
    (begun,) = call(
        functools.partial(early_kernel, lags // 2),
        [whole],
        [pl.ANY] * 2,
        [pltpu.SemaphoreType.DMA],
        out_specs=[pl.ANY],
    )(*early)
    (out,) = call(
        functools.partial(late_kernel, lags // 2),
        [whole],
        [pl.ANY] * 3,
        [pltpu.SemaphoreType.DMA],
        out_specs=[pl.ANY],
        aliases={0: 0},
    )(begun, *late)
    return out


def solution(mesh):
    in_specs = (
        P("lag", "patch", None),
        P("lag", "patch", None),
        P("patch", None),
        P("patch", None),
        P("patch", None),
        P("patch"),
        P("patch", None, None),
    )
    out_specs = P(None, "patch", None)

    return jax.shard_map(local, mesh=mesh, in_specs=in_specs, out_specs=out_specs, check_vma=False)
```

```python
import functools

import jax
import jax.numpy as jnp
from jax import lax
from jax.experimental import pallas as pl
from jax.experimental.pallas import tpu as pltpu
from jax.sharding import PartitionSpec as P

NEAR = 5
CAP = 16
HALF = NEAR // 2
LANES = 128
VMEM = pltpu.VMEM


def dot(left, right):
    return jnp.dot(left, right, preferred_element_type=jnp.float32)


def slot_offsets(patch):
    odd = lax.rem(patch, 2)
    high = lax.rem(lax.div(patch, 2), 2)
    return [4 * high, 1 + 2 * odd, 4 - 4 * high, 3 - 2 * odd, HALF]


def pairings(patches):
    far = [(i + 2 if i & 2 else i - 2) % patches for i in range(patches)]
    odd_even = [(i + 1 if i & 1 else i - 1) % patches for i in range(patches)]
    near = [i ^ 2 for i in range(patches)]
    core = [i ^ 1 for i in range(patches)]
    return [list(enumerate(p)) for p in (far, odd_even, near, core)]


def pack_kernel(tile_hbm, panel_hbm, history, rows_ref, out_ref, edge, tile_ref, panel_ref, sems):
    copies = [
        pltpu.make_async_copy(tile_hbm, tile_ref, sems.at[0]),
        pltpu.make_async_copy(panel_hbm, panel_ref, sems.at[1]),
        pltpu.make_async_copy(
            history.at[pl.ds(history.shape[0] - edge.shape[0], edge.shape[0])], edge, sems.at[2]
        ),
    ]
    for copy in copies:
        copy.start()
    for copy in copies[:2]:
        copy.wait()
    recv = rows_ref.shape[0]
    width = rows_ref.shape[1]
    slots = out_ref.shape[0]
    patches = slots // CAP
    tile = tile_ref[...]
    hot = lax.broadcasted_iota(jnp.int32, (patches, recv), 0) == tile
    before = lax.broadcasted_iota(jnp.int32, (recv, recv), 0) < lax.broadcasted_iota(
        jnp.int32, (recv, recv), 1
    )
    hot = jnp.where(hot, 1.0, 0.0)
    ahead = dot(hot.astype(jnp.bfloat16), jnp.where(before, 1.0, 0.0).astype(jnp.bfloat16))
    earlier = jnp.sum(hot * ahead, axis=0, keepdims=True).astype(jnp.int32)
    slot = tile * CAP + earlier
    placed = lax.broadcasted_iota(jnp.int32, (slots, recv), 0) == slot
    placer = jnp.where(placed, 1.0, 0.0).astype(jnp.bfloat16)
    out_ref[:, :width] = dot(placer, rows_ref[...]).astype(jnp.bfloat16)
    marks = jnp.where(placed, (panel_ref[...] + 1).astype(jnp.float32), 0.0)
    label = jnp.sum(marks, axis=1, keepdims=True)
    out_ref[:, width:] = jnp.broadcast_to(label, (slots, LANES)).astype(jnp.bfloat16)
    copies[2].wait()


def source_kernel(arrived_ref, *outs):
    slots = arrived_ref.shape[0]
    shots, tile_len = outs[0].shape
    width = len(outs) * shots
    label = arrived_ref[:, width:].astype(jnp.float32)
    lane = lax.broadcasted_iota(jnp.int32, (slots, LANES), 1)
    picker = jnp.concatenate(
        [
            jnp.where(label == (lane + (1 + first)).astype(jnp.float32), 1.0, 0.0)
            for first in range(0, tile_len, LANES)
        ],
        axis=1,
    ).astype(jnp.bfloat16)
    for step, out in enumerate(outs):
        out[...] = lax.dot_general(
            arrived_ref[:, step * shots : (step + 1) * shots],
            picker,
            (((0,), (0,)), ((), ())),
            preferred_element_type=jnp.float32,
        )


def older_kernel(steps, sizes, ranges, rim, history, inverse_hbm, weights, *refs):
    outs, (rows, blocks, sems, out_sems) = refs[:-4], refs[-4:]
    messages, outs = outs[: NEAR - 1], outs[NEAR - 1 :]
    own, stage, recent, inverse = outs[:4]
    rest = outs[4:]
    band, tile_len, shots = history.shape
    lag = lax.axis_index("lag")
    offsets = slot_offsets(lax.axis_index("patch"))

    def bounds(offset):
        base = lag * band + 1
        first = jnp.clip(ranges[0, offset] - base, 0, band)
        last = jnp.clip(ranges[0, NEAR + offset] - base, 0, band)
        return first, last

    def fetch(slot, offset, k):
        columns = pl.ds(pl.multiple_of(offset * tile_len, tile_len), tile_len)
        return pltpu.make_async_copy(
            weights.at[k, :, columns], blocks.at[slot, k], sems.at[slot, k]
        )

    def send(slot, step, target):
        return pltpu.make_async_copy(
            stage.at[slot, pl.ds(step * shots, shots)], target, out_sems.at[slot, step]
        )

    for slot, offset in enumerate(offsets):
        first, last = bounds(offset)
        lax.fori_loop(first, last, lambda k, c, s=slot, o=offset: fetch(s, o, k).start(), None)
    keep = [
        pltpu.make_async_copy(weights.at[pl.ds(0, steps - 1)], recent, out_sems.at[NEAR, 0]),
        pltpu.make_async_copy(inverse_hbm, inverse, out_sems.at[NEAR, 1]),
    ]
    for copy in keep:
        copy.start()
    for k in range(band):
        rows[(band - 1 - k) * shots : (band - k) * shots, :] = history[k].T

    @pl.when(lag > 0)
    def _():
        for k in range(steps - 1):
            at = (band + steps - 2 - k) * shots
            rows[at : at + shots, :] = rim[k].T

    @pl.when(lag == 0)
    def _():
        rows[band * shots :, :] = jnp.zeros(((steps - 1) * shots, tile_len), jnp.bfloat16)

    def window(k):
        return rows[pl.ds(pl.multiple_of((band - 1 - k) * shots, shots), steps * shots), :]

    def one_slot(slot, carry):
        offset = offsets[-1]
        for j in range(NEAR - 1):
            offset = jnp.where(slot == j, offsets[j], offset)
        first, last = bounds(offset)
        lax.fori_loop(first, last, lambda k, c: fetch(slot, offset, k).wait(), None)

        def emit(total):
            stage[slot] = total.astype(jnp.bfloat16)

            @pl.when(slot == NEAR - 1)
            def _():
                own[...] = total[:shots]

        def branch(size):
            def run():
                start = jnp.minimum(first, band - size)
                left, right = [], []
                for i in range(size):
                    k = start + i
                    live = (k >= first) & (k < last)
                    tile = blocks[slot, k]
                    left.append(window(k))
                    right.append(jnp.where(live, tile, jnp.zeros_like(tile)))
                emit(dot(jnp.concatenate(left, axis=1), jnp.concatenate(right, axis=0)))

            return run

        count = last - first
        which = jnp.where(count > 0, 1, 0)
        for i, size in enumerate(sizes[:-1]):
            which = jnp.where(count > size, i + 2, which)
        lax.switch(
            which,
            [lambda: emit(jnp.zeros((steps * shots, tile_len), jnp.float32))]
            + [branch(size) for size in sizes],
        )
        for j in range(NEAR - 1):
            pl.when(slot == j)(lambda j=j: send(j, 0, messages[j]).start())
        for step in range(1, steps):
            send(slot, step, rest[step - 1].at[pl.ds(slot * shots, shots)]).start()
        return carry

    lax.fori_loop(0, NEAR, one_slot, None)
    for copy in keep:
        copy.wait()
    for slot in range(NEAR):
        if slot < NEAR - 1:
            send(slot, 0, messages[slot]).wait()
        for step in range(1, steps):
            send(slot, step, rest[step - 1].at[pl.ds(slot * shots, shots)]).wait()


def step_kernel(step, last_step, ranges, source, inverse, own, *refs):
    shots = own.shape[0]
    tile_len = own.shape[1]
    refs = list(refs)
    received = [refs.pop(0) for _ in range(1 if step == 0 else NEAR - 1)]
    right = source[...] - own[...]
    for block in received:
        right = right - block[...].astype(jnp.float32)
    density = dot(right.astype(jnp.bfloat16), inverse[...])
    if last_step:
        (natural,) = refs
        natural[...] = density.T.astype(jnp.bfloat16)
        return
    weights, stage, rest_far = refs[:3]
    olders, outs = refs[3 : 3 + step], refs[3 + step :]
    density_ref, next_own = outs[:2]
    messages = outs[2:]
    rounded = density.astype(jnp.bfloat16)
    density_ref[...] = rounded
    band_zero = lax.axis_index("lag") == 0
    recent = [rounded] + [ref[...] for ref in olders]
    nxt = step + 1
    for slot, offset in enumerate(slot_offsets(lax.axis_index("patch"))):
        terms = stage[slot, nxt * shots : (nxt + 1) * shots, :].astype(jnp.float32)
        terms = terms + rest_far[slot * shots : (slot + 1) * shots, :].astype(jnp.float32)
        columns = pl.ds(pl.multiple_of(offset * tile_len, tile_len), tile_len)
        for k, block in enumerate(recent):
            lag = k + 1
            live = band_zero & (ranges[0, offset] <= lag) & (lag < ranges[0, NEAR + offset])
            scale = jnp.where(live, 1.0, 0.0).astype(jnp.float32)
            terms = terms + scale * dot(block, weights[k, :, columns])
        if slot < NEAR - 1:
            messages[slot][...] = terms.astype(jnp.bfloat16)
        else:
            next_own[...] = terms


def natural_kernel(*refs):
    blocks, out = refs[:-1], refs[-1]
    for k, block in enumerate(blocks):
        out[k] = block[...].astype(jnp.float32).T.astype(jnp.bfloat16)


def early_kernel(near_lags, mine, far, out, sem):
    def move(block):
        copy = pltpu.make_async_copy(block, out.at[pl.ds(0, block.shape[0])], sem)
        copy.start()
        copy.wait()

    keeps = lax.axis_index("lag") < near_lags
    pl.when(keeps)(lambda: move(mine))
    pl.when(jnp.logical_not(keeps))(lambda: move(far))


def late_kernel(near_lags, begun, mine, far, out, sem):
    del begun

    def move(block):
        copy = pltpu.make_async_copy(block, out.at[out.shape[0] - 1], sem)
        copy.start()
        copy.wait()

    keeps = lax.axis_index("lag") < near_lags
    pl.when(keeps)(lambda: move(mine))
    pl.when(jnp.logical_not(keeps))(lambda: move(far))


def call(kernel, outs, specs, scratch=(), out_specs=None, aliases=None, limit=8 << 20):
    made = []
    for shape, dtype, *space in outs:
        made.append(space[0](shape, dtype) if space else jax.ShapeDtypeStruct(shape, dtype))
    return pl.pallas_call(
        kernel,
        out_shape=made,
        in_specs=[pl.BlockSpec(memory_space=space) for space in specs],
        out_specs=[pl.BlockSpec(memory_space=s) for s in (out_specs or [VMEM] * len(made))],
        scratch_shapes=list(scratch),
        input_output_aliases=aliases or {},
        compiler_params=pltpu.CompilerParams(vmem_limit_bytes=limit),
    )


def near_memory(array):
    return pltpu.with_memory_space_constraint(array, VMEM)


def far_memory(array):
    return pltpu.with_memory_space_constraint(array, pltpu.HBM)


def lag_partners(lags, distance):
    return [(i, i ^ distance) for i in range(lags)]


def lag_sum(block, lags):
    far, distance = None, 1
    while distance < lags:
        if far is not None:
            block = block + far.astype(block.dtype)
        far = lax.ppermute(block.astype(jnp.bfloat16), "lag", lag_partners(lags, distance))
        distance *= 2
    return block, far


def from_band_zero(block, lags):
    index = lax.axis_index("lag")
    distance = 1
    far = block
    while distance < lags:
        if distance > 1:
            block = jnp.where(index < distance // 2, block, far)
        far = lax.ppermute(block, "lag", lag_partners(lags, distance))
        distance *= 2
    return block, far


def local(interaction, history, near_inverse, lag_ranges, receiver_tile, receiver_panel, residuals):
    tile_len = near_inverse.shape[1]
    band, _, shots = history.shape
    recv, steps, _ = residuals.shape
    patches, lags = lax.axis_size("patch"), lax.axis_size("lag")
    width = steps * shots
    f32, bf16 = jnp.float32, jnp.bfloat16
    block = (shots, tile_len)
    routes = pairings(patches)

    outgoing, edge = call(
        pack_kernel,
        [((patches * CAP, width + LANES), bf16), ((steps - 1, tile_len, shots), bf16)],
        [pltpu.HBM] * 3 + [VMEM],
        [VMEM((1, recv), jnp.int32)] * 2 + [pltpu.SemaphoreType.DMA((3,))],
        out_specs=[VMEM, pl.ANY],
    )(
        far_memory(receiver_tile.reshape(1, recv)),
        far_memory(receiver_panel.reshape(1, recv)),
        far_memory(history),
        residuals.reshape(recv, width),
    )
    rim = lax.ppermute(edge, "lag", [(i, (i + 1) % lags) for i in range(lags)])
    arrived = lax.all_to_all(
        outgoing.reshape(patches, CAP, width + LANES),
        "patch",
        split_axis=0,
        concat_axis=0,
        tiled=True,
    ).reshape(patches * CAP, width + LANES)
    source = call(source_kernel, [(block, f32, VMEM)] * steps, [VMEM])(arrived)
    source = [near_memory(s) for s in source]

    sizes = [*range(2, band, 2), band]
    older = call(
        functools.partial(older_kernel, steps, sizes),
        [(block, bf16)] * (NEAR - 1)
        + [
            (block, f32, VMEM),
            ((NEAR, width, tile_len), bf16, VMEM),
            ((steps - 1, tile_len, NEAR * tile_len), bf16, VMEM),
            ((tile_len, tile_len), bf16, VMEM),
        ]
        + [((NEAR * shots, tile_len), bf16)] * (steps - 1),
        [pltpu.SMEM, VMEM, VMEM, pltpu.HBM, pltpu.HBM],
        [
            VMEM(((band + steps - 1) * shots, tile_len), bf16),
            VMEM((NEAR, band, tile_len, tile_len), bf16),
            pltpu.SemaphoreType.DMA((NEAR, band)),
            pltpu.SemaphoreType.DMA((NEAR + 1, steps)),
        ],
        out_specs=[pl.ANY] * (NEAR - 1) + [VMEM] * 4 + [pl.ANY] * (steps - 1),
        limit=54 << 20,
    )(lag_ranges, rim, history, far_memory(near_inverse), far_memory(interaction))
    messages, (own, stage, recent, inverse), rest = older[: NEAR - 1], older[NEAR - 1 : NEAR + 3], older[NEAR + 3 :]
    stage, recent, inverse = near_memory(stage), near_memory(recent), near_memory(inverse)

    def exchange(blocks):
        gone = []
        for b, r in zip(blocks, routes):
            gone.append(lax.ppermute(b, "patch", r))
        return gone

    for incoming in exchange(messages):
        own = own + incoming.astype(f32)
    own, far = lag_sum(own, lags)
    received = [far]
    pairs = []
    for r in rest:
        pairs.append(lag_sum(r, lags))

    densities = []
    for step in range(steps):
        last_step = step == steps - 1
        inputs = [lag_ranges, source[step], inverse, own, *received]
        if last_step:
            outs = [((tile_len, shots), bf16)]
        else:
            here, there = pairs[step]
            if lags > 2:
                there = there + (here - rest[step])
            inputs += [recent, stage, there, *densities[::-1]]
            outs = [(block, bf16, VMEM), (block, f32, VMEM)] + [(block, bf16)] * (NEAR - 1)
        results = call(
            functools.partial(step_kernel, step, last_step),
            outs,
            [pltpu.SMEM] + [VMEM] * (len(inputs) - 1),
        )(*inputs)
        if not last_step:
            densities.append(near_memory(results[0]))
            own = near_memory(results[1])
            received = exchange(results[2:])
    (early,) = call(
        natural_kernel, [((steps - 1, tile_len, shots), bf16)], [VMEM] * (steps - 1)
    )(*densities)
    early = from_band_zero(early, lags)
    late = from_band_zero(results[0], lags)
    whole = ((steps, tile_len, shots), bf16)
    (begun,) = call(
        functools.partial(early_kernel, lags // 2),
        [whole],
        [pl.ANY] * 2,
        [pltpu.SemaphoreType.DMA],
        out_specs=[pl.ANY],
    )(*early)
    (out,) = call(
        functools.partial(late_kernel, lags // 2),
        [whole],
        [pl.ANY] * 3,
        [pltpu.SemaphoreType.DMA],
        out_specs=[pl.ANY],
        aliases={0: 0},
    )(begun, *late)
    return out


def solution(mesh):
    in_specs = (
        P("lag", "patch", None),
        P("lag", "patch", None),
        P("patch", None),
        P("patch", None),
        P("patch", None),
        P("patch"),
        P("patch", None, None),
    )
    out_specs = P(None, "patch", None)

    return jax.shard_map(local, mesh=mesh, in_specs=in_specs, out_specs=out_specs, check_vma=False)
```

```python
import functools

import jax
import jax.numpy as jnp
from jax import lax
from jax.experimental import pallas as pl
from jax.experimental.pallas import tpu as pltpu
from jax.sharding import PartitionSpec as P

NEAR = 5
CAP = 16
HALF = NEAR // 2
LANES = 128
VMEM = pltpu.VMEM


def dot(left, right):
    return jnp.dot(left, right, preferred_element_type=jnp.float32)


def slot_offsets(patch):
    odd = lax.rem(patch, 2)
    high = lax.rem(lax.div(patch, 2), 2)
    return [4 * high, 1 + 2 * odd, 4 - 4 * high, 3 - 2 * odd, HALF]


def pairings(patches):
    far = [(i + 2 if i & 2 else i - 2) % patches for i in range(patches)]
    odd_even = [(i + 1 if i & 1 else i - 1) % patches for i in range(patches)]
    near = [i ^ 2 for i in range(patches)]
    core = [i ^ 1 for i in range(patches)]
    return [list(enumerate(p)) for p in (far, odd_even, near, core)]


def pack_kernel(tile_hbm, panel_hbm, history, rows_ref, out_ref, edge, tile_ref, panel_ref, sems):
    copies = [
        pltpu.make_async_copy(tile_hbm, tile_ref, sems.at[0]),
        pltpu.make_async_copy(panel_hbm, panel_ref, sems.at[1]),
        pltpu.make_async_copy(
            history.at[pl.ds(history.shape[0] - edge.shape[0], edge.shape[0])], edge, sems.at[2]
        ),
    ]
    for copy in copies:
        copy.start()
    for copy in copies[:2]:
        copy.wait()
    recv = rows_ref.shape[0]
    width = rows_ref.shape[1]
    slots = out_ref.shape[0]
    patches = slots // CAP
    tile = tile_ref[...]
    hot = lax.broadcasted_iota(jnp.int32, (patches, recv), 0) == tile
    before = lax.broadcasted_iota(jnp.int32, (recv, recv), 0) < lax.broadcasted_iota(
        jnp.int32, (recv, recv), 1
    )
    hot = jnp.where(hot, 1.0, 0.0)
    ahead = dot(hot.astype(jnp.bfloat16), jnp.where(before, 1.0, 0.0).astype(jnp.bfloat16))
    earlier = jnp.sum(hot * ahead, axis=0, keepdims=True).astype(jnp.int32)
    slot = tile * CAP + earlier
    placed = lax.broadcasted_iota(jnp.int32, (slots, recv), 0) == slot
    placer = jnp.where(placed, 1.0, 0.0).astype(jnp.bfloat16)
    out_ref[:, :width] = dot(placer, rows_ref[...]).astype(jnp.bfloat16)
    marks = jnp.where(placed, (panel_ref[...] + 1).astype(jnp.float32), 0.0)
    label = jnp.sum(marks, axis=1, keepdims=True)
    out_ref[:, width:] = jnp.broadcast_to(label, (slots, LANES)).astype(jnp.bfloat16)
    copies[2].wait()


def source_kernel(arrived_ref, *outs):
    slots = arrived_ref.shape[0]
    shots, tile_len = outs[0].shape
    width = len(outs) * shots
    label = arrived_ref[:, width:].astype(jnp.float32)
    lane = lax.broadcasted_iota(jnp.int32, (slots, LANES), 1)
    picker = jnp.concatenate(
        [
            jnp.where(label == (lane + (1 + first)).astype(jnp.float32), 1.0, 0.0)
            for first in range(0, tile_len, LANES)
        ],
        axis=1,
    ).astype(jnp.bfloat16)
    for step, out in enumerate(outs):
        out[...] = lax.dot_general(
            arrived_ref[:, step * shots : (step + 1) * shots],
            picker,
            (((0,), (0,)), ((), ())),
            preferred_element_type=jnp.float32,
        )


def older_kernel(steps, sizes, ranges, rim, history, inverse_hbm, weights, *refs):
    outs, (rows, blocks, sems, out_sems) = refs[:-4], refs[-4:]
    messages, outs = outs[: NEAR - 1], outs[NEAR - 1 :]
    own, stage, recent, inverse = outs[:4]
    (rest,) = outs[4:]
    band, tile_len, shots = history.shape
    lag = lax.axis_index("lag")
    offsets = slot_offsets(lax.axis_index("patch"))

    def bounds(offset):
        base = lag * band + 1
        first = jnp.clip(ranges[0, offset] - base, 0, band)
        last = jnp.clip(ranges[0, NEAR + offset] - base, 0, band)
        return first, last

    def fetch(slot, offset, k):
        columns = pl.ds(pl.multiple_of(offset * tile_len, tile_len), tile_len)
        return pltpu.make_async_copy(
            weights.at[k, :, columns], blocks.at[slot, k], sems.at[slot, k]
        )

    def send(slot, step, target):
        return pltpu.make_async_copy(
            stage.at[slot, pl.ds(step * shots, shots)], target, out_sems.at[slot, step]
        )

    for slot, offset in enumerate(offsets):
        first, last = bounds(offset)
        lax.fori_loop(first, last, lambda k, c, s=slot, o=offset: fetch(s, o, k).start(), None)
    keep = [
        pltpu.make_async_copy(weights.at[pl.ds(0, steps - 1)], recent, out_sems.at[NEAR, 0]),
        pltpu.make_async_copy(inverse_hbm, inverse, out_sems.at[NEAR, 1]),
    ]
    for copy in keep:
        copy.start()
    for k in range(band):
        rows[(band - 1 - k) * shots : (band - k) * shots, :] = history[k].T

    @pl.when(lag > 0)
    def _():
        for k in range(steps - 1):
            at = (band + steps - 2 - k) * shots
            rows[at : at + shots, :] = rim[k].T

    @pl.when(lag == 0)
    def _():
        rows[band * shots :, :] = jnp.zeros(((steps - 1) * shots, tile_len), jnp.bfloat16)

    def window(k):
        return rows[pl.ds(pl.multiple_of((band - 1 - k) * shots, shots), steps * shots), :]

    def one_slot(slot, carry):
        offset = offsets[-1]
        for j in range(NEAR - 1):
            offset = jnp.where(slot == j, offsets[j], offset)
        first, last = bounds(offset)
        lax.fori_loop(first, last, lambda k, c: fetch(slot, offset, k).wait(), None)

        def emit(total):
            stage[slot] = total.astype(jnp.bfloat16)

            @pl.when(slot == NEAR - 1)
            def _():
                own[...] = total[:shots]

        def branch(size):
            def run():
                start = jnp.minimum(first, band - size)
                left, right = [], []
                for i in range(size):
                    k = start + i
                    live = (k >= first) & (k < last)
                    tile = blocks[slot, k]
                    left.append(window(k))
                    right.append(jnp.where(live, tile, jnp.zeros_like(tile)))
                emit(dot(jnp.concatenate(left, axis=1), jnp.concatenate(right, axis=0)))

            return run

        count = last - first
        which = jnp.where(count > 0, 1, 0)
        for i, size in enumerate(sizes[:-1]):
            which = jnp.where(count > size, i + 2, which)
        lax.switch(
            which,
            [lambda: emit(jnp.zeros((steps * shots, tile_len), jnp.float32))]
            + [branch(size) for size in sizes],
        )
        for j in range(NEAR - 1):
            pl.when(slot == j)(lambda j=j: send(j, 0, messages[j]).start())
        send(slot, 1, rest.at[pl.ds(slot * shots, shots)]).start()
        return carry

    lax.fori_loop(0, NEAR, one_slot, None)
    for copy in keep:
        copy.wait()
    for slot in range(NEAR):
        if slot < NEAR - 1:
            send(slot, 0, messages[slot]).wait()
        send(slot, 1, rest.at[pl.ds(slot * shots, shots)]).wait()


def step_kernel(step, last_step, ranges, source, inverse, own, *refs):
    shots, tile_len = own.shape
    refs = list(refs)
    received = [refs.pop(0) for _ in range(NEAR - 1 if step > 0 else 0)]
    total = own[...]
    for block in received:
        total = total + block[...].astype(jnp.float32)
    right = source[...] - total
    if step != 1:
        right = right - refs.pop(0)[...].astype(jnp.float32)
    density = dot(right.astype(jnp.bfloat16), inverse[...])
    rounded = density.astype(jnp.bfloat16)
    if last_step:
        refs[0][...] = rounded
        return
    weights, stage = refs[:2]
    rest_far = refs[2] if step == 0 else None
    refs = refs[3 if step == 0 else 2 :]
    olders, outs = refs[:step], refs[step:]
    density_ref, cross, next_own = outs[:3]
    messages = outs[3:]
    band_zero = lax.axis_index("lag") == 0
    density_ref[...] = rounded
    cross[...] = jnp.where(band_zero, density, total).astype(jnp.bfloat16)
    recent = [rounded] + [ref[...] for ref in olders]
    steps = stage.shape[1] // shots
    ahead = jnp.where(band_zero, step + 1, min(step + 2, steps - 1))
    rows = pl.ds(pl.multiple_of(ahead * shots, shots), shots)
    for slot, offset in enumerate(slot_offsets(lax.axis_index("patch"))):
        terms = stage[slot, rows, :].astype(jnp.float32)
        if step == 0:
            there = rest_far[slot * shots : (slot + 1) * shots, :].astype(jnp.float32)
            terms = terms + jnp.where(band_zero, there, 0.0)
        columns = pl.ds(pl.multiple_of(offset * tile_len, tile_len), tile_len)
        for k, block in enumerate(recent):
            lag = k + 1
            live = band_zero & (ranges[0, offset] <= lag) & (lag < ranges[0, NEAR + offset])
            scale = jnp.where(live, 1.0, 0.0).astype(jnp.float32)
            terms = terms + scale * dot(block, weights[k, :, columns])
        if slot < NEAR - 1:
            messages[slot][...] = terms.astype(jnp.bfloat16)
        else:
            next_own[...] = terms


def begin_kernel(near_lags, *refs):
    count = (len(refs) - 3) // 2
    mine, far, (out, rows, sem) = refs[:count], refs[count : 2 * count], refs[2 * count :]
    keeps = lax.axis_index("lag") < near_lags
    for k in range(count):
        block = jnp.where(keeps, mine[k][...], far[k][...])
        rows[k] = block.astype(jnp.float32).T.astype(jnp.bfloat16)
    copy = pltpu.make_async_copy(rows, out.at[pl.ds(0, count)], sem)
    copy.start()
    copy.wait()


def finish_kernel(near_lags, begun, mine, far, out, rows, sem):
    del begun
    block = jnp.where(lax.axis_index("lag") < near_lags, mine[...], far[...])
    rows[...] = block.astype(jnp.float32).T.astype(jnp.bfloat16)
    copy = pltpu.make_async_copy(rows, out.at[out.shape[0] - 1], sem)
    copy.start()
    copy.wait()


def call(kernel, outs, specs, scratch=(), out_specs=None, aliases=None, limit=8 << 20):
    made = []
    for shape, dtype, *space in outs:
        made.append(space[0](shape, dtype) if space else jax.ShapeDtypeStruct(shape, dtype))
    return pl.pallas_call(
        kernel,
        out_shape=made,
        in_specs=[pl.BlockSpec(memory_space=space) for space in specs],
        out_specs=[pl.BlockSpec(memory_space=s) for s in (out_specs or [VMEM] * len(made))],
        scratch_shapes=list(scratch),
        input_output_aliases=aliases or {},
        compiler_params=pltpu.CompilerParams(vmem_limit_bytes=limit),
    )


def near_memory(array):
    return pltpu.with_memory_space_constraint(array, VMEM)


def far_memory(array):
    return pltpu.with_memory_space_constraint(array, pltpu.HBM)


def lag_partners(lags, distance):
    return [(i, i ^ distance) for i in range(lags)]


def lag_sum(block, lags):
    far, distance = None, 1
    while distance < lags:
        if far is not None:
            block = block + far.astype(block.dtype)
        far = lax.ppermute(block.astype(jnp.bfloat16), "lag", lag_partners(lags, distance))
        distance *= 2
    return block, far


def from_band_zero(block, lags):
    index = lax.axis_index("lag")
    distance = 1
    far = block
    while distance < lags:
        if distance > 1:
            block = jnp.where(index < distance // 2, block, far)
        far = lax.ppermute(block, "lag", lag_partners(lags, distance))
        distance *= 2
    return block, far


def local(interaction, history, near_inverse, lag_ranges, receiver_tile, receiver_panel, residuals):
    tile_len = near_inverse.shape[1]
    band, _, shots = history.shape
    recv, steps, _ = residuals.shape
    patches, lags = lax.axis_size("patch"), lax.axis_size("lag")
    width = steps * shots
    f32, bf16 = jnp.float32, jnp.bfloat16
    block = (shots, tile_len)
    routes = pairings(patches)

    outgoing, edge = call(
        pack_kernel,
        [((patches * CAP, width + LANES), bf16), ((steps - 1, tile_len, shots), bf16)],
        [pltpu.HBM] * 3 + [VMEM],
        [VMEM((1, recv), jnp.int32)] * 2 + [pltpu.SemaphoreType.DMA((3,))],
        out_specs=[VMEM, pl.ANY],
    )(
        far_memory(receiver_tile.reshape(1, recv)),
        far_memory(receiver_panel.reshape(1, recv)),
        far_memory(history),
        residuals.reshape(recv, width),
    )
    rim = lax.ppermute(edge, "lag", [(i, (i + 1) % lags) for i in range(lags)])
    arrived = lax.all_to_all(
        outgoing.reshape(patches, CAP, width + LANES),
        "patch",
        split_axis=0,
        concat_axis=0,
        tiled=True,
    ).reshape(patches * CAP, width + LANES)
    source = call(source_kernel, [(block, f32, VMEM)] * steps, [VMEM])(arrived)
    source = [near_memory(s) for s in source]

    sizes = [*range(2, band, 2), band]
    older = call(
        functools.partial(older_kernel, steps, sizes),
        [(block, bf16)] * (NEAR - 1)
        + [
            (block, f32, VMEM),
            ((NEAR, width, tile_len), bf16, VMEM),
            ((steps - 1, tile_len, NEAR * tile_len), bf16, VMEM),
            ((tile_len, tile_len), bf16, VMEM),
        ]
        + [((NEAR * shots, tile_len), bf16)],
        [pltpu.SMEM, VMEM, VMEM, pltpu.HBM, pltpu.HBM],
        [
            VMEM(((band + steps - 1) * shots, tile_len), bf16),
            VMEM((NEAR, band, tile_len, tile_len), bf16),
            pltpu.SemaphoreType.DMA((NEAR, band)),
            pltpu.SemaphoreType.DMA((NEAR + 1, steps)),
        ],
        out_specs=[pl.ANY] * (NEAR - 1) + [VMEM] * 4 + [pl.ANY],
        limit=54 << 20,
    )(lag_ranges, rim, history, far_memory(near_inverse), far_memory(interaction))
    messages, (own, stage, recent, inverse, rest) = older[: NEAR - 1], older[NEAR - 1 :]
    stage, recent, inverse = near_memory(stage), near_memory(recent), near_memory(inverse)

    def exchange(blocks):
        gone = []
        for b, r in zip(blocks, routes):
            gone.append(lax.ppermute(b, "patch", r))
        return gone

    for incoming in exchange(messages):
        own = own + incoming.astype(f32)
    own, far = lag_sum(own, lags)
    here, there = lag_sum(rest, lags)
    if lags > 2:
        there = there + (here - rest)

    def cross_bands(block):
        if lags == 2:
            swapped = lax.ppermute(block, "lag", lag_partners(lags, 1))
            return (block, swapped), swapped
        outward = from_band_zero(block, lags)
        inward, last = lag_sum(jnp.where(lax.axis_index("lag") > 0, block, 0), lags)
        return outward, inward + last

    densities, outward, inward = [], [], [far]
    received = []
    for step in range(steps):
        last_step = step == steps - 1
        inputs = [lag_ranges, source[step], inverse, own, *received]
        if step != 1:
            inputs.append(inward[max(step - 1, 0)])
        outs = [(block, bf16)]
        if not last_step:
            inputs += [recent, stage] + [there] * (step == 0) + densities[::-1]
            outs = [(block, bf16, VMEM), (block, bf16), (block, f32, VMEM)]
            outs += [(block, bf16)] * (NEAR - 1)
        results = call(
            functools.partial(step_kernel, step, last_step),
            outs,
            [pltpu.SMEM] + [VMEM] * (len(inputs) - 1),
        )(*inputs)
        if last_step:
            ends, _ = cross_bands(results[0])
        else:
            densities.append(near_memory(results[0]))
            sent, back = cross_bands(results[1])
            outward.append(sent)
            if step == 0:
                inward = [far]
            else:
                inward.append(back)
            own = near_memory(results[2])
            received = exchange(results[3:])
    whole = ((steps, tile_len, shots), bf16)
    pairs = [mine for mine, _ in outward] + [theirs for _, theirs in outward]
    (begun,) = call(
        functools.partial(begin_kernel, lags // 2),
        [whole],
        [VMEM] * len(pairs),
        [VMEM((steps - 1, tile_len, shots), bf16), pltpu.SemaphoreType.DMA],
        out_specs=[pl.ANY],
    )(*pairs)
    (out,) = call(
        functools.partial(finish_kernel, lags // 2),
        [whole],
        [pl.ANY, VMEM, VMEM],
        [VMEM((tile_len, shots), bf16), pltpu.SemaphoreType.DMA],
        out_specs=[pl.ANY],
        aliases={0: 0},
    )(begun, *ends)
    return out


def solution(mesh):
    in_specs = (
        P("lag", "patch", None),
        P("lag", "patch", None),
        P("patch", None),
        P("patch", None),
        P("patch", None),
        P("patch"),
        P("patch", None, None),
    )
    out_specs = P(None, "patch", None)

    return jax.shard_map(local, mesh=mesh, in_specs=in_specs, out_specs=out_specs, check_vma=False)
```

```python
import functools

import jax
import jax.numpy as jnp
from jax import lax
from jax.experimental import pallas as pl
from jax.experimental.pallas import tpu as pltpu
from jax.sharding import PartitionSpec as P

NEAR = 5
CAP = 16
HALF = NEAR // 2
FIRST = 2
LANES = 128
VMEM = pltpu.VMEM
FAR_LIMIT = 40 << 20
NEAR_LIMIT = 40 << 20


def dot(left, right):
    return jnp.dot(left, right, preferred_element_type=jnp.float32)


def slot_offsets(patch):
    odd = lax.rem(patch, 2)
    high = lax.rem(lax.div(patch, 2), 2)
    return [4 * high, 1 + 2 * odd, 4 - 4 * high, 3 - 2 * odd, HALF]


def pairings(patches):
    far = [(i + 2 if i & 2 else i - 2) % patches for i in range(patches)]
    odd_even = [(i + 1 if i & 1 else i - 1) % patches for i in range(patches)]
    near = [i ^ 2 for i in range(patches)]
    core = [i ^ 1 for i in range(patches)]
    return [list(enumerate(p)) for p in (far, odd_even, near, core)]


def pack_kernel(tile_hbm, panel_hbm, history, rows_ref, out_ref, edge, tile_ref, panel_ref, sems):
    copies = [
        pltpu.make_async_copy(tile_hbm, tile_ref, sems.at[0]),
        pltpu.make_async_copy(panel_hbm, panel_ref, sems.at[1]),
        pltpu.make_async_copy(
            history.at[pl.ds(history.shape[0] - edge.shape[0], edge.shape[0])], edge, sems.at[2]
        ),
    ]
    for copy in copies:
        copy.start()
    for copy in copies[:2]:
        copy.wait()
    recv = rows_ref.shape[0]
    width = rows_ref.shape[1]
    slots = out_ref.shape[0]
    patches = slots // CAP
    tile = tile_ref[...]
    hot = lax.broadcasted_iota(jnp.int32, (patches, recv), 0) == tile
    before = lax.broadcasted_iota(jnp.int32, (recv, recv), 0) < lax.broadcasted_iota(
        jnp.int32, (recv, recv), 1
    )
    hot = jnp.where(hot, 1.0, 0.0)
    ahead = dot(hot.astype(jnp.bfloat16), jnp.where(before, 1.0, 0.0).astype(jnp.bfloat16))
    earlier = jnp.sum(hot * ahead, axis=0, keepdims=True).astype(jnp.int32)
    slot = tile * CAP + earlier
    placed = lax.broadcasted_iota(jnp.int32, (slots, recv), 0) == slot
    placer = jnp.where(placed, 1.0, 0.0).astype(jnp.bfloat16)
    out_ref[:, :width] = dot(placer, rows_ref[...]).astype(jnp.bfloat16)
    marks = jnp.where(placed, (panel_ref[...] + 1).astype(jnp.float32), 0.0)
    label = jnp.sum(marks, axis=1, keepdims=True)
    out_ref[:, width:] = jnp.broadcast_to(label, (slots, LANES)).astype(jnp.bfloat16)
    copies[2].wait()


def source_kernel(arrived_ref, *outs):
    slots = arrived_ref.shape[0]
    shots, tile_len = outs[0].shape
    width = len(outs) * shots
    label = arrived_ref[:, width:].astype(jnp.float32)
    lane = lax.broadcasted_iota(jnp.int32, (slots, LANES), 1)
    picker = jnp.concatenate(
        [
            jnp.where(label == (lane + (1 + first)).astype(jnp.float32), 1.0, 0.0)
            for first in range(0, tile_len, LANES)
        ],
        axis=1,
    ).astype(jnp.bfloat16)
    for step, out in enumerate(outs):
        out[...] = lax.dot_general(
            arrived_ref[:, step * shots : (step + 1) * shots],
            picker,
            (((0,), (0,)), ((), ())),
            preferred_element_type=jnp.float32,
        )


def active(ranges, offset, lag, band):
    base = lag * band + 1
    first = jnp.clip(ranges[0, offset] - base, 0, band)
    last = jnp.clip(ranges[0, NEAR + offset] - base, 0, band)
    return first, last


def history_terms(ranges, slots, sizes, shots, rows, blocks, stage, arrive, emitted):
    _, width, tile_len = stage.shape
    band = blocks.shape[1]
    lag = lax.axis_index("lag")
    offsets = slot_offsets(lax.axis_index("patch"))

    def window(k):
        return rows[pl.ds(pl.multiple_of((band - 1 - k) * shots, shots), width), :]

    def one_slot(index, carry):
        offset = offsets[slots[-1]]
        for i, slot in enumerate(slots[:-1]):
            offset = jnp.where(index == i, offsets[slot], offset)
        first, last = active(ranges, offset, lag, band)
        arrive(index, first, last, offset)

        def emit(total):
            stage[index] = total.astype(jnp.bfloat16)
            emitted(index, total)

        def branch(size):
            def run():
                start = jnp.minimum(first, band - size)
                left, right = [], []
                for i in range(size):
                    k = start + i
                    live = (k >= first) & (k < last)
                    tile = blocks[index, k]
                    left.append(window(k))
                    right.append(jnp.where(live, tile, jnp.zeros_like(tile)))
                emit(dot(jnp.concatenate(left, axis=1), jnp.concatenate(right, axis=0)))

            return run

        count = last - first
        which = jnp.where(count > 0, 1, 0)
        for i, size in enumerate(sizes[:-1]):
            which = jnp.where(count > size, i + 2, which)
        lax.switch(
            which,
            [lambda: emit(jnp.zeros((width, tile_len), jnp.float32))]
            + [branch(size) for size in sizes],
        )
        return carry

    lax.fori_loop(0, len(slots), one_slot, None)


def far_kernel(steps, sizes, ranges, rim, history_hbm, inverse_hbm, weights, *refs):
    far_message, odd_message, stage, rows, later, recent, inverse = refs[:7]
    blocks, history, sems, keep_sems, out_sems = refs[7:]
    band, tile_len, shots = history.shape
    lag = lax.axis_index("lag")
    offsets = slot_offsets(lax.axis_index("patch"))

    def fetch(slot, offset, k):
        columns = pl.ds(pl.multiple_of(offset * tile_len, tile_len), tile_len)
        place = blocks.at[slot, k] if slot < FIRST else later.at[slot - FIRST, k]
        return pltpu.make_async_copy(weights.at[k, :, columns], place, sems.at[slot, k])

    keep = [
        pltpu.make_async_copy(history_hbm, history, keep_sems.at[0]),
        pltpu.make_async_copy(weights.at[pl.ds(0, steps - 1)], recent, keep_sems.at[1]),
        pltpu.make_async_copy(inverse_hbm, inverse, keep_sems.at[2]),
    ]
    keep[0].start()
    for slot, offset in enumerate(offsets):
        first, last = active(ranges, offset, lag, band)
        lax.fori_loop(first, last, lambda k, c, s=slot, o=offset: fetch(s, o, k).start(), None)
    keep[1].start()
    keep[2].start()
    keep[0].wait()
    for k in range(band):
        rows[(band - 1 - k) * shots : (band - k) * shots, :] = history[k].T

    @pl.when(lag > 0)
    def _():
        for k in range(steps - 1):
            at = (band + steps - 2 - k) * shots
            rows[at : at + shots, :] = rim[k].T

    @pl.when(lag == 0)
    def _():
        rows[band * shots :, :] = jnp.zeros(((steps - 1) * shots, tile_len), jnp.bfloat16)

    def arrive(index, first, last, offset):
        def wait(k, carry):
            columns = pl.ds(pl.multiple_of(offset * tile_len, tile_len), tile_len)
            pltpu.make_async_copy(
                weights.at[k, :, columns], blocks.at[index, k], sems.at[index, k]
            ).wait()
            return carry

        lax.fori_loop(first, last, wait, None)

    targets = (far_message, odd_message)

    def send(index):
        return pltpu.make_async_copy(
            stage.at[index, pl.ds(0, shots)], targets[index], out_sems.at[index]
        )

    def emitted(index, total):
        for i in range(FIRST):
            pl.when(index == i)(lambda i=i: send(i).start())

    history_terms(ranges, range(FIRST), sizes, shots, rows, blocks, stage, arrive, emitted)
    for slot in range(FIRST, NEAR):
        first, last = active(ranges, offsets[slot], lag, band)
        lax.fori_loop(first, last, lambda k, c, s=slot: fetch(s, offsets[s], k).wait(), None)
    keep[1].wait()
    keep[2].wait()
    for index in range(FIRST):
        send(index).wait()


def near_kernel(sizes, ranges, rows, blocks, far_stage, *refs):
    near_message, core_message, own, stage, rest, out_sems = refs
    shots = own.shape[0]
    targets = (near_message, core_message)

    def pass_on(slot):
        held = far_stage.at[slot] if slot < FIRST else stage.at[slot - FIRST]
        return pltpu.make_async_copy(
            held.at[pl.ds(shots, shots)], rest.at[pl.ds(slot * shots, shots)], out_sems.at[0, slot]
        )

    def send(index):
        return pltpu.make_async_copy(
            stage.at[index, pl.ds(0, shots)], targets[index], out_sems.at[1, index]
        )

    for slot in range(FIRST):
        pass_on(slot).start()

    def emitted(index, total):
        for i in range(NEAR - FIRST):

            @pl.when(index == i)
            def _(i=i):
                pass_on(FIRST + i).start()
                if i < len(targets):
                    send(i).start()
                else:
                    own[...] = total[:shots]

    history_terms(
        ranges, range(FIRST, NEAR), sizes, shots, rows, blocks, stage, lambda *_: None, emitted
    )
    for slot in range(NEAR):
        pass_on(slot).wait()
    for index in range(len(targets)):
        send(index).wait()


def step_kernel(step, last_step, ranges, source, inverse, own, *refs):
    shots, tile_len = own.shape
    refs = list(refs)
    received = [refs.pop(0) for _ in range(NEAR - 1 if step > 0 else 0)]
    total = own[...]
    for block in received:
        total = total + block[...].astype(jnp.float32)
    right = source[...] - total
    if step != 1:
        right = right - refs.pop(0)[...].astype(jnp.float32)
    density = dot(right.astype(jnp.bfloat16), inverse[...])
    rounded = density.astype(jnp.bfloat16)
    if last_step:
        refs[0][...] = rounded
        return
    weights, far_stage, near_stage = refs[:3]
    rest_far = refs[3] if step == 0 else None
    refs = refs[4 if step == 0 else 3 :]
    olders, outs = refs[:step], refs[step:]
    cross, next_own = outs[:2]
    messages = outs[2 : NEAR + 1]
    band_zero = lax.axis_index("lag") == 0
    for density_ref in outs[NEAR + 1 :]:
        density_ref[...] = rounded
    cross[...] = jnp.where(band_zero, density, total).astype(jnp.bfloat16)
    recent = [rounded] + [ref[...] for ref in olders]
    steps = far_stage.shape[1] // shots
    ahead = jnp.where(band_zero, step + 1, min(step + 2, steps - 1))
    rows = pl.ds(pl.multiple_of(ahead * shots, shots), shots)
    for slot, offset in enumerate(slot_offsets(lax.axis_index("patch"))):
        held = far_stage.at[slot] if slot < FIRST else near_stage.at[slot - FIRST]
        terms = held[rows, :].astype(jnp.float32)
        if step == 0:
            there = rest_far[slot * shots : (slot + 1) * shots, :].astype(jnp.float32)
            terms = terms + jnp.where(band_zero, there, 0.0)
        columns = pl.ds(pl.multiple_of(offset * tile_len, tile_len), tile_len)
        for k, block in enumerate(recent):
            lag = k + 1
            live = band_zero & (ranges[0, offset] <= lag) & (lag < ranges[0, NEAR + offset])
            scale = jnp.where(live, 1.0, 0.0).astype(jnp.float32)
            terms = terms + scale * dot(block, weights[k, :, columns])
        if slot < NEAR - 1:
            messages[slot][...] = terms.astype(jnp.bfloat16)
        else:
            next_own[...] = terms


def begin_kernel(near_lags, *refs):
    count = (len(refs) - 3) // 2
    mine, far, (out, rows, sem) = refs[:count], refs[count : 2 * count], refs[2 * count :]
    keeps = lax.axis_index("lag") < near_lags
    for k in range(count):
        block = jnp.where(keeps, mine[k][...], far[k][...])
        rows[k] = block.astype(jnp.float32).T.astype(jnp.bfloat16)
    copy = pltpu.make_async_copy(rows, out.at[pl.ds(0, count)], sem)
    copy.start()
    copy.wait()


def finish_kernel(near_lags, begun, mine, far, out, rows, sem):
    del begun
    block = jnp.where(lax.axis_index("lag") < near_lags, mine[...], far[...])
    rows[...] = block.astype(jnp.float32).T.astype(jnp.bfloat16)
    copy = pltpu.make_async_copy(rows, out.at[out.shape[0] - 1], sem)
    copy.start()
    copy.wait()


def call(kernel, outs, specs, scratch=(), out_specs=None, aliases=None, limit=8 << 20):
    made = []
    for shape, dtype, *space in outs:
        made.append(space[0](shape, dtype) if space else jax.ShapeDtypeStruct(shape, dtype))
    return pl.pallas_call(
        kernel,
        out_shape=made,
        in_specs=[pl.BlockSpec(memory_space=space) for space in specs],
        out_specs=[pl.BlockSpec(memory_space=s) for s in (out_specs or [VMEM] * len(made))],
        scratch_shapes=list(scratch),
        input_output_aliases=aliases or {},
        compiler_params=pltpu.CompilerParams(vmem_limit_bytes=limit),
    )


def near_memory(array):
    return pltpu.with_memory_space_constraint(array, VMEM)


def far_memory(array):
    return pltpu.with_memory_space_constraint(array, pltpu.HBM)


def lag_partners(lags, distance):
    return [(i, i ^ distance) for i in range(lags)]


def lag_sum(block, lags):
    far, distance = None, 1
    while distance < lags:
        if far is not None:
            block = block + far.astype(block.dtype)
        far = lax.ppermute(block.astype(jnp.bfloat16), "lag", lag_partners(lags, distance))
        distance *= 2
    return block, far


def from_band_zero(block, lags):
    index = lax.axis_index("lag")
    distance = 1
    far = block
    while distance < lags:
        if distance > 1:
            block = jnp.where(index < distance // 2, block, far)
        far = lax.ppermute(block, "lag", lag_partners(lags, distance))
        distance *= 2
    return block, far


def local(interaction, history, near_inverse, lag_ranges, receiver_tile, receiver_panel, residuals):
    tile_len = near_inverse.shape[1]
    band, _, shots = history.shape
    recv, steps, _ = residuals.shape
    patches, lags = lax.axis_size("patch"), lax.axis_size("lag")
    width = steps * shots
    f32, bf16 = jnp.float32, jnp.bfloat16
    block = (shots, tile_len)
    routes = pairings(patches)

    outgoing, edge = call(
        pack_kernel,
        [((patches * CAP, width + LANES), bf16), ((steps - 1, tile_len, shots), bf16)],
        [pltpu.HBM] * 3 + [VMEM],
        [VMEM((1, recv), jnp.int32)] * 2 + [pltpu.SemaphoreType.DMA((3,))],
        out_specs=[VMEM, pl.ANY],
    )(
        far_memory(receiver_tile.reshape(1, recv)),
        far_memory(receiver_panel.reshape(1, recv)),
        far_memory(history),
        residuals.reshape(recv, width),
    )
    rim = lax.ppermute(edge, "lag", [(i, (i + 1) % lags) for i in range(lags)])
    arrived = lax.all_to_all(
        outgoing.reshape(patches, CAP, width + LANES),
        "patch",
        split_axis=0,
        concat_axis=0,
        tiled=True,
    ).reshape(patches * CAP, width + LANES)
    source = call(source_kernel, [(block, f32, VMEM)] * steps, [VMEM])(arrived)
    source = [near_memory(s) for s in source]

    sizes = [*range(2, band, 2), band]
    older_rows = ((band + steps - 1) * shots, tile_len)
    *first, far_stage, rows, later, recent, inverse = call(
        functools.partial(far_kernel, steps, sizes),
        [(block, bf16, pltpu.HBM)] * FIRST
        + [
            ((FIRST, width, tile_len), bf16, VMEM),
            (older_rows, bf16, VMEM),
            ((NEAR - FIRST, band, tile_len, tile_len), bf16, VMEM),
            ((steps - 1, tile_len, NEAR * tile_len), bf16, VMEM),
            ((tile_len, tile_len), bf16, VMEM),
        ],
        [pltpu.SMEM, VMEM] + [pltpu.HBM] * 3,
        [
            VMEM((FIRST, band, tile_len, tile_len), bf16),
            VMEM((band, tile_len, shots), bf16),
            pltpu.SemaphoreType.DMA((NEAR, band)),
            pltpu.SemaphoreType.DMA((3,)),
            pltpu.SemaphoreType.DMA((FIRST,)),
        ],
        out_specs=[pltpu.HBM] * FIRST + [VMEM] * 5,
        limit=FAR_LIMIT,
    )(far_memory(lag_ranges), rim, far_memory(history), far_memory(near_inverse), far_memory(interaction))
    far_stage, rows, later = near_memory(far_stage), near_memory(rows), near_memory(later)
    recent, inverse = near_memory(recent), near_memory(inverse)
    *second, own, near_stage, rest = call(
        functools.partial(near_kernel, sizes),
        [(block, bf16, pltpu.HBM)] * (NEAR - 1 - FIRST)
        + [
            (block, f32),
            ((NEAR - FIRST, width, tile_len), bf16, VMEM),
            ((NEAR * shots, tile_len), bf16, pltpu.HBM),
        ],
        [pltpu.SMEM] + [VMEM] * 3,
        [pltpu.SemaphoreType.DMA((2, NEAR))],
        out_specs=[pltpu.HBM] * (NEAR - 1 - FIRST) + [VMEM] * 2 + [pltpu.HBM],
        limit=NEAR_LIMIT,
    )(lag_ranges, rows, later, far_stage)
    near_stage = near_memory(near_stage)
    messages = [*first, *second]

    def exchange(blocks):
        gone = []
        for b, r in zip(blocks, routes):
            gone.append(lax.ppermute(b, "patch", r))
        return gone

    for incoming in exchange(messages):
        own = own + incoming.astype(f32)
    own, far = lag_sum(own, lags)
    here, there = lag_sum(rest, lags)
    if lags > 2:
        there = there + (here - rest)

    def cross_bands(block):
        if lags == 2:
            swapped = lax.ppermute(block, "lag", lag_partners(lags, 1))
            return (block, swapped), swapped
        outward = from_band_zero(block, lags)
        inward, last = lag_sum(jnp.where(lax.axis_index("lag") > 0, block, 0), lags)
        return outward, inward + last

    densities, outward, inward = [], [], [far]
    received = []
    for step in range(steps):
        last_step = step == steps - 1
        inputs = [lag_ranges, source[step], inverse, own, *received]
        if step != 1:
            inputs.append(inward[max(step - 1, 0)])
        outs = [(block, bf16)]
        if not last_step:
            inputs += [recent, far_stage, near_stage] + [there] * (step == 0) + densities[::-1]
            outs = [(block, bf16), (block, f32, VMEM)] + [(block, bf16)] * (NEAR - 1)
            outs += [(block, bf16, VMEM)] * (step < steps - 2)
        results = call(
            functools.partial(step_kernel, step, last_step),
            outs,
            [pltpu.SMEM] + [VMEM] * (len(inputs) - 1),
        )(*inputs)
        if last_step:
            ends, _ = cross_bands(results[0])
        else:
            densities += [near_memory(r) for r in results[NEAR + 1 :]]
            sent, back = cross_bands(results[0])
            outward.append(sent)
            if step == 0:
                inward = [far]
            else:
                inward.append(back)
            own = near_memory(results[1])
            received = exchange(results[2 : NEAR + 1])
    whole = ((steps, tile_len, shots), bf16)
    pairs = [mine for mine, _ in outward] + [theirs for _, theirs in outward]
    (begun,) = call(
        functools.partial(begin_kernel, lags // 2),
        [whole],
        [VMEM] * len(pairs),
        [VMEM((steps - 1, tile_len, shots), bf16), pltpu.SemaphoreType.DMA],
        out_specs=[pl.ANY],
    )(*pairs)
    (out,) = call(
        functools.partial(finish_kernel, lags // 2),
        [whole],
        [pl.ANY, VMEM, VMEM],
        [VMEM((tile_len, shots), bf16), pltpu.SemaphoreType.DMA],
        out_specs=[pl.ANY],
        aliases={0: 0},
    )(begun, *ends)
    return out


def solution(mesh):
    in_specs = (
        P("lag", "patch", None),
        P("lag", "patch", None),
        P("patch", None),
        P("patch", None),
        P("patch", None),
        P("patch"),
        P("patch", None, None),
    )
    out_specs = P(None, "patch", None)

    return jax.shard_map(local, mesh=mesh, in_specs=in_specs, out_specs=out_specs, check_vma=False)
```

```python
import functools

import jax
import jax.numpy as jnp
from jax import lax
from jax.experimental import pallas as pl
from jax.experimental.pallas import tpu as pltpu
from jax.sharding import PartitionSpec as P

NEAR = 5
CAP = 16
HALF = NEAR // 2
PIECES = 2
LIMIT = 46 << 20
LANES = 128
VMEM = pltpu.VMEM


def dot(left, right):
    return jnp.dot(left, right, preferred_element_type=jnp.float32)


def slot_offsets(patch):
    odd = lax.rem(patch, 2)
    high = lax.rem(lax.div(patch, 2), 2)
    return [4 * high, 1 + 2 * odd, 4 - 4 * high, 3 - 2 * odd, HALF]


def pairings(patches):
    far = [(i + 2 if i & 2 else i - 2) % patches for i in range(patches)]
    odd_even = [(i + 1 if i & 1 else i - 1) % patches for i in range(patches)]
    near = [i ^ 2 for i in range(patches)]
    core = [i ^ 1 for i in range(patches)]
    return [list(enumerate(p)) for p in (far, odd_even, near, core)]


def pack_kernel(tile_hbm, panel_hbm, rows_ref, out_hbm, tile_ref, panel_ref, sems, out_ref, out_sem):
    copies = [
        pltpu.make_async_copy(tile_hbm, tile_ref, sems.at[0]),
        pltpu.make_async_copy(panel_hbm, panel_ref, sems.at[1]),
    ]
    for copy in copies:
        copy.start()
    for copy in copies:
        copy.wait()
    recv = rows_ref.shape[0]
    slots, width = out_ref.shape
    width = width - LANES
    patches = slots // CAP
    tile = tile_ref[...]
    hot = lax.broadcasted_iota(jnp.int32, (patches, recv), 0) == tile
    before = lax.broadcasted_iota(jnp.int32, (recv, recv), 0) < lax.broadcasted_iota(
        jnp.int32, (recv, recv), 1
    )
    hot = jnp.where(hot, 1.0, 0.0)
    ahead = dot(hot.astype(jnp.bfloat16), jnp.where(before, 1.0, 0.0).astype(jnp.bfloat16))
    earlier = jnp.sum(hot * ahead, axis=0, keepdims=True).astype(jnp.int32)
    slot = tile * CAP + earlier
    placed = lax.broadcasted_iota(jnp.int32, (slots, recv), 0) == slot
    placer = jnp.where(placed, 1.0, 0.0).astype(jnp.bfloat16)
    piece = lax.rem(lax.axis_index("lag"), rows_ref.shape[1] // width)
    rows = rows_ref[:, pl.ds(pl.multiple_of(piece * width, width), width)]
    out_ref[:, :width] = dot(placer, rows).astype(jnp.bfloat16)
    marks = jnp.where(placed, (panel_ref[...] + 1).astype(jnp.float32), 0.0)
    label = jnp.sum(marks, axis=1, keepdims=True)
    out_ref[:, width:] = jnp.broadcast_to(label, (slots, LANES)).astype(jnp.bfloat16)
    copy = pltpu.make_async_copy(out_ref, out_hbm, out_sem)
    copy.start()
    copy.wait()


def source_kernel(shots, arrived_ref, out):
    slots = arrived_ref.shape[0]
    width, tile_len = out.shape
    label = arrived_ref[:, width:].astype(jnp.float32)
    lane = lax.broadcasted_iota(jnp.int32, (slots, LANES), 1)
    picker = jnp.concatenate(
        [
            jnp.where(label == (lane + (1 + first)).astype(jnp.float32), 1.0, 0.0)
            for first in range(0, tile_len, LANES)
        ],
        axis=1,
    ).astype(jnp.bfloat16)
    for first in range(0, width, shots):
        out[first : first + shots, :] = lax.dot_general(
            arrived_ref[:, first : first + shots],
            picker,
            (((0,), (0,)), ((), ())),
            preferred_element_type=jnp.float32,
        )


def older_kernel(steps, sizes, ranges, rim, history, inverse_hbm, weights, *refs):
    outs, (rows, blocks, sems, out_sems) = refs[:-4], refs[-4:]
    messages, outs = outs[: NEAR - 1], outs[NEAR - 1 :]
    own, stage, recent, inverse = outs[:4]
    (rest,) = outs[4:]
    band, tile_len, shots = history.shape
    lag = lax.axis_index("lag")
    offsets = slot_offsets(lax.axis_index("patch"))

    def bounds(offset):
        base = lag * band + 1
        first = jnp.clip(ranges[0, offset] - base, 0, band)
        last = jnp.clip(ranges[0, NEAR + offset] - base, 0, band)
        return first, last

    def fetch(slot, offset, k):
        columns = pl.ds(pl.multiple_of(offset * tile_len, tile_len), tile_len)
        return pltpu.make_async_copy(
            weights.at[k, :, columns], blocks.at[slot, k], sems.at[slot, k]
        )

    def send(slot, step, target):
        return pltpu.make_async_copy(
            stage.at[slot, pl.ds(step * shots, shots)], target, out_sems.at[slot, step]
        )

    for slot, offset in enumerate(offsets):
        first, last = bounds(offset)
        lax.fori_loop(first, last, lambda k, c, s=slot, o=offset: fetch(s, o, k).start(), None)
    keep = [
        pltpu.make_async_copy(weights.at[pl.ds(0, steps - 1)], recent, out_sems.at[NEAR, 0]),
        pltpu.make_async_copy(inverse_hbm, inverse, out_sems.at[NEAR, 1]),
    ]
    for copy in keep:
        copy.start()
    for k in range(band):
        rows[(band - 1 - k) * shots : (band - k) * shots, :] = history[k].T

    @pl.when(lag > 0)
    def _():
        for k in range(steps - 1):
            at = (band + steps - 2 - k) * shots
            rows[at : at + shots, :] = rim[k].T

    @pl.when(lag == 0)
    def _():
        rows[band * shots :, :] = jnp.zeros(((steps - 1) * shots, tile_len), jnp.bfloat16)

    def window(k):
        return rows[pl.ds(pl.multiple_of((band - 1 - k) * shots, shots), steps * shots), :]

    def one_slot(slot, carry):
        offset = offsets[-1]
        for j in range(NEAR - 1):
            offset = jnp.where(slot == j, offsets[j], offset)
        first, last = bounds(offset)
        lax.fori_loop(first, last, lambda k, c: fetch(slot, offset, k).wait(), None)

        def emit(total):
            stage[slot] = total.astype(jnp.bfloat16)

            @pl.when(slot == NEAR - 1)
            def _():
                own[...] = total[:shots]

        def branch(size):
            def run():
                start = jnp.minimum(first, band - size)
                left, right = [], []
                for i in range(size):
                    k = start + i
                    live = (k >= first) & (k < last)
                    tile = blocks[slot, k]
                    left.append(window(k))
                    right.append(jnp.where(live, tile, jnp.zeros_like(tile)))
                emit(dot(jnp.concatenate(left, axis=1), jnp.concatenate(right, axis=0)))

            return run

        count = last - first
        which = jnp.where(count > 0, 1, 0)
        for i, size in enumerate(sizes[:-1]):
            which = jnp.where(count > size, i + 2, which)
        lax.switch(
            which,
            [lambda: emit(jnp.zeros((steps * shots, tile_len), jnp.float32))]
            + [branch(size) for size in sizes],
        )
        for j in range(NEAR - 1):
            pl.when(slot == j)(lambda j=j: send(j, 0, messages[j]).start())
        send(slot, 1, rest.at[pl.ds(slot * shots, shots)]).start()
        return carry

    lax.fori_loop(0, NEAR, one_slot, None)
    for copy in keep:
        copy.wait()
    for slot in range(NEAR):
        if slot < NEAR - 1:
            send(slot, 0, messages[slot]).wait()
        send(slot, 1, rest.at[pl.ds(slot * shots, shots)]).wait()


def sum_kernel(own, *refs):
    *blocks, half = refs
    total = own[...]
    for block in blocks:
        total = total + block[...].astype(jnp.float32)
    half[...] = total.astype(jnp.bfloat16)


def step_kernel(step, last_step, ranges, source, inverse, own, *refs):
    shots, tile_len = own.shape
    refs = list(refs)
    received = [refs.pop(0) for _ in range(NEAR - 1)]
    total = own[...]
    for block in received:
        total = total + block[...].astype(jnp.float32)
    held = source.shape[0] // shots
    right = source[step * shots : (step + 1) * shots, :] - total if step < held else -total
    if step != 1:
        right = right - refs.pop(0)[...].astype(jnp.float32)
    density = dot(right.astype(jnp.bfloat16), inverse[...])
    rounded = density.astype(jnp.bfloat16)
    if last_step:
        refs[0][...] = rounded
        return
    weights, stage = refs[:2]
    rest_far = refs[2] if step == 0 else None
    refs = refs[3 if step == 0 else 2 :]
    olders, outs = refs[:step], refs[step:]
    density_ref, cross, next_own = outs[:3]
    messages = outs[3:]
    band_zero = lax.axis_index("lag") == 0
    density_ref[...] = rounded
    if step + 1 >= held:
        at = (step + 1 - held) * shots
        carried = jnp.where(lax.axis_index("lag") == 1, source[at : at + shots, :], 0.0)
        total = total - carried
    cross[...] = jnp.where(band_zero, density, total).astype(jnp.bfloat16)
    recent = [rounded] + [ref[...] for ref in olders]
    steps = stage.shape[1] // shots
    ahead = jnp.where(band_zero, step + 1, min(step + 2, steps - 1))
    rows = pl.ds(pl.multiple_of(ahead * shots, shots), shots)
    for slot, offset in enumerate(slot_offsets(lax.axis_index("patch"))):
        terms = stage[slot, rows, :].astype(jnp.float32)
        if step == 0:
            there = rest_far[slot * shots : (slot + 1) * shots, :].astype(jnp.float32)
            terms = terms + jnp.where(band_zero, there, 0.0)
        columns = pl.ds(pl.multiple_of(offset * tile_len, tile_len), tile_len)
        for k, block in enumerate(recent):
            lag = k + 1
            live = band_zero & (ranges[0, offset] <= lag) & (lag < ranges[0, NEAR + offset])
            scale = jnp.where(live, 1.0, 0.0).astype(jnp.float32)
            terms = terms + scale * dot(block, weights[k, :, columns])
        if slot < NEAR - 1:
            messages[slot][...] = terms.astype(jnp.bfloat16)
        else:
            next_own[...] = terms


def begin_kernel(near_lags, *refs):
    count = (len(refs) - 3) // 2
    mine, far, (out, rows, sem) = refs[:count], refs[count : 2 * count], refs[2 * count :]
    keeps = lax.axis_index("lag") < near_lags
    for k in range(count):
        block = jnp.where(keeps, mine[k][...], far[k][...])
        rows[k] = block.astype(jnp.float32).T.astype(jnp.bfloat16)
    copy = pltpu.make_async_copy(rows, out.at[pl.ds(0, count)], sem)
    copy.start()
    copy.wait()


def finish_kernel(near_lags, begun, mine, far, out, rows, sem):
    del begun
    block = jnp.where(lax.axis_index("lag") < near_lags, mine[...], far[...])
    rows[...] = block.astype(jnp.float32).T.astype(jnp.bfloat16)
    copy = pltpu.make_async_copy(rows, out.at[out.shape[0] - 1], sem)
    copy.start()
    copy.wait()


def call(kernel, outs, specs, scratch=(), out_specs=None, aliases=None, limit=8 << 20):
    made = []
    for shape, dtype, *space in outs:
        made.append(space[0](shape, dtype) if space else jax.ShapeDtypeStruct(shape, dtype))
    return pl.pallas_call(
        kernel,
        out_shape=made,
        in_specs=[pl.BlockSpec(memory_space=space) for space in specs],
        out_specs=[pl.BlockSpec(memory_space=s) for s in (out_specs or [VMEM] * len(made))],
        scratch_shapes=list(scratch),
        input_output_aliases=aliases or {},
        compiler_params=pltpu.CompilerParams(vmem_limit_bytes=limit),
    )


def near_memory(array):
    return pltpu.with_memory_space_constraint(array, VMEM)


def far_memory(array):
    return pltpu.with_memory_space_constraint(array, pltpu.HBM)


def lag_partners(lags, distance):
    return [(i, i ^ distance) for i in range(lags)]


def lag_sum(block, lags):
    far, distance = None, 1
    while distance < lags:
        if far is not None:
            block = block + far.astype(block.dtype)
        far = lax.ppermute(block.astype(jnp.bfloat16), "lag", lag_partners(lags, distance))
        distance *= 2
    return block, far


def from_band_zero(block, lags):
    index = lax.axis_index("lag")
    distance = 1
    far = block
    while distance < lags:
        if distance > 1:
            block = jnp.where(index < distance // 2, block, far)
        far = lax.ppermute(block, "lag", lag_partners(lags, distance))
        distance *= 2
    return block, far


def local(interaction, history, near_inverse, lag_ranges, receiver_tile, receiver_panel, residuals):
    tile_len = near_inverse.shape[1]
    band, _, shots = history.shape
    recv, steps, _ = residuals.shape
    patches, lags = lax.axis_size("patch"), lax.axis_size("lag")
    width = steps * shots
    f32, bf16 = jnp.float32, jnp.bfloat16
    block = (shots, tile_len)
    routes = pairings(patches)
    piece = width // PIECES

    piece = width // PIECES
    rim = lax.ppermute(
        history[band - steps + 1 :], "lag", [(i, (i + 1) % lags) for i in range(lags)]
    )
    (outgoing,) = call(
        pack_kernel,
        [((patches * CAP, piece + LANES), bf16, pltpu.HBM)],
        [pltpu.HBM] * 2 + [VMEM],
        [VMEM((1, recv), jnp.int32)] * 2 + [pltpu.SemaphoreType.DMA((2,))]
        + [VMEM((patches * CAP, piece + LANES), bf16), pltpu.SemaphoreType.DMA],
        out_specs=[pltpu.HBM],
    )(
        far_memory(receiver_tile.reshape(1, recv)),
        far_memory(receiver_panel.reshape(1, recv)),
        residuals.reshape(recv, width),
    )
    arrived = lax.all_to_all(
        outgoing.reshape(patches, CAP, piece + LANES),
        "patch",
        split_axis=0,
        concat_axis=0,
        tiled=True,
    ).reshape(patches * CAP, piece + LANES)
    (source,) = call(
        functools.partial(source_kernel, shots), [((piece, tile_len), f32, VMEM)], [VMEM]
    )(arrived)
    source = near_memory(source)

    sizes = [*range(2, band, 2), band]
    older = call(
        functools.partial(older_kernel, steps, sizes),
        [(block, bf16, pltpu.HBM)] * (NEAR - 1)
        + [
            (block, f32, VMEM),
            ((NEAR, width, tile_len), bf16, VMEM),
            ((steps - 1, tile_len, NEAR * tile_len), bf16, VMEM),
            ((tile_len, tile_len), bf16, VMEM),
        ]
        + [((NEAR * shots, tile_len), bf16, pltpu.HBM)],
        [pltpu.SMEM, VMEM, VMEM, pltpu.HBM, pltpu.HBM],
        [
            VMEM(((band + steps - 1) * shots, tile_len), bf16),
            VMEM((NEAR, band, tile_len, tile_len), bf16),
            pltpu.SemaphoreType.DMA((NEAR, band)),
            pltpu.SemaphoreType.DMA((NEAR + 1, steps)),
        ],
        out_specs=[pltpu.HBM] * (NEAR - 1) + [VMEM] * 4 + [pltpu.HBM],
        limit=LIMIT,
    )(far_memory(lag_ranges), rim, history, far_memory(near_inverse), far_memory(interaction))
    messages, (own, stage, recent, inverse, rest) = older[: NEAR - 1], older[NEAR - 1 :]
    stage, recent, inverse = near_memory(stage), near_memory(recent), near_memory(inverse)

    def exchange(blocks):
        gone = []
        for b, r in zip(blocks, routes):
            gone.append(lax.ppermute(b, "patch", r))
        return gone

    own = near_memory(own)
    received = exchange(messages)
    (half,) = call(sum_kernel, [(block, bf16)], [VMEM] * NEAR)(own, *received)
    if lags > 2:
        half = lag_sum(jnp.where(lax.axis_index("lag") > 0, half, 0), lags)
        far = half[0] + half[1]
    else:
        far = lax.ppermute(half, "lag", lag_partners(lags, 1))
    here, there = lag_sum(rest, lags)
    if lags > 2:
        there = there + (here - rest)

    def cross_bands(block):
        if lags == 2:
            swapped = lax.ppermute(block, "lag", lag_partners(lags, 1))
            return (block, swapped), swapped
        outward = from_band_zero(block, lags)
        inward, last = lag_sum(jnp.where(lax.axis_index("lag") > 0, block, 0), lags)
        return outward, inward + last

    densities, outward, inward = [], [], [far]
    for step in range(steps):
        last_step = step == steps - 1
        inputs = [lag_ranges, source, inverse, own, *received]
        if step != 1:
            inputs.append(inward[max(step - 1, 0)])
        outs = [(block, bf16)]
        if not last_step:
            inputs += [recent, stage] + [there] * (step == 0) + densities[::-1]
            outs = [(block, bf16, VMEM), (block, bf16), (block, f32, VMEM)]
            outs += [(block, bf16)] * (NEAR - 1)
        results = call(
            functools.partial(step_kernel, step, last_step),
            outs,
            [pltpu.SMEM] + [VMEM] * (len(inputs) - 1),
        )(*inputs)
        if last_step:
            ends, _ = cross_bands(results[0])
        else:
            densities.append(near_memory(results[0]))
            sent, back = cross_bands(results[1])
            outward.append(sent)
            if step == 0:
                inward = [far]
            else:
                inward.append(back)
            own = near_memory(results[2])
            received = exchange(results[3:])
    whole = ((steps, tile_len, shots), bf16)
    pairs = [mine for mine, _ in outward] + [theirs for _, theirs in outward]
    (begun,) = call(
        functools.partial(begin_kernel, lags // 2),
        [whole],
        [VMEM] * len(pairs),
        [VMEM((steps - 1, tile_len, shots), bf16), pltpu.SemaphoreType.DMA],
        out_specs=[pl.ANY],
    )(*pairs)
    (out,) = call(
        functools.partial(finish_kernel, lags // 2),
        [whole],
        [pl.ANY, VMEM, VMEM],
        [VMEM((tile_len, shots), bf16), pltpu.SemaphoreType.DMA],
        out_specs=[pl.ANY],
        aliases={0: 0},
    )(begun, *ends)
    return out


def solution(mesh):
    in_specs = (
        P("lag", "patch", None),
        P("lag", "patch", None),
        P("patch", None),
        P("patch", None),
        P("patch", None),
        P("patch"),
        P("patch", None, None),
    )
    out_specs = P(None, "patch", None)

    return jax.shard_map(local, mesh=mesh, in_specs=in_specs, out_specs=out_specs, check_vma=False)
```

```python
import functools

import jax
import jax.numpy as jnp
from jax import lax
from jax.experimental import pallas as pl
from jax.experimental.pallas import tpu as pltpu
from jax.sharding import PartitionSpec as P

NEAR = 5
CAP = 16
HALF = NEAR // 2
FIRST = 2
PIECES = 2
LANES = 128
VMEM = pltpu.VMEM
FAR_LIMIT = 40 << 20
NEAR_LIMIT = 40 << 20


def dot(left, right):
    return jnp.dot(left, right, preferred_element_type=jnp.float32)


def slot_offsets(patch):
    odd = lax.rem(patch, 2)
    high = lax.rem(lax.div(patch, 2), 2)
    return [4 * high, 1 + 2 * odd, 4 - 4 * high, 3 - 2 * odd, HALF]


def pairings(patches):
    far = [(i + 2 if i & 2 else i - 2) % patches for i in range(patches)]
    odd_even = [(i + 1 if i & 1 else i - 1) % patches for i in range(patches)]
    near = [i ^ 2 for i in range(patches)]
    core = [i ^ 1 for i in range(patches)]
    return [list(enumerate(p)) for p in (far, odd_even, near, core)]


def pack_kernel(tile_hbm, panel_hbm, rows_ref, out_hbm, tile_ref, panel_ref, sems, out_ref, out_sem):
    copies = [
        pltpu.make_async_copy(tile_hbm, tile_ref, sems.at[0]),
        pltpu.make_async_copy(panel_hbm, panel_ref, sems.at[1]),
    ]
    for copy in copies:
        copy.start()
    for copy in copies:
        copy.wait()
    recv = rows_ref.shape[0]
    slots, width = out_ref.shape
    width = width - LANES
    patches = slots // CAP
    tile = tile_ref[...]
    hot = lax.broadcasted_iota(jnp.int32, (patches, recv), 0) == tile
    before = lax.broadcasted_iota(jnp.int32, (recv, recv), 0) < lax.broadcasted_iota(
        jnp.int32, (recv, recv), 1
    )
    hot = jnp.where(hot, 1.0, 0.0)
    ahead = dot(hot.astype(jnp.bfloat16), jnp.where(before, 1.0, 0.0).astype(jnp.bfloat16))
    earlier = jnp.sum(hot * ahead, axis=0, keepdims=True).astype(jnp.int32)
    slot = tile * CAP + earlier
    placed = lax.broadcasted_iota(jnp.int32, (slots, recv), 0) == slot
    placer = jnp.where(placed, 1.0, 0.0).astype(jnp.bfloat16)
    piece = lax.rem(lax.axis_index("lag"), rows_ref.shape[1] // width)
    rows = rows_ref[:, pl.ds(pl.multiple_of(piece * width, width), width)]
    out_ref[:, :width] = dot(placer, rows).astype(jnp.bfloat16)
    marks = jnp.where(placed, (panel_ref[...] + 1).astype(jnp.float32), 0.0)
    label = jnp.sum(marks, axis=1, keepdims=True)
    out_ref[:, width:] = jnp.broadcast_to(label, (slots, LANES)).astype(jnp.bfloat16)
    copy = pltpu.make_async_copy(out_ref, out_hbm, out_sem)
    copy.start()
    copy.wait()


def source_kernel(shots, arrived_ref, out):
    slots = arrived_ref.shape[0]
    width, tile_len = out.shape
    label = arrived_ref[:, width:].astype(jnp.float32)
    lane = lax.broadcasted_iota(jnp.int32, (slots, LANES), 1)
    picker = jnp.concatenate(
        [
            jnp.where(label == (lane + (1 + first)).astype(jnp.float32), 1.0, 0.0)
            for first in range(0, tile_len, LANES)
        ],
        axis=1,
    ).astype(jnp.bfloat16)
    for first in range(0, width, shots):
        out[first : first + shots, :] = lax.dot_general(
            arrived_ref[:, first : first + shots],
            picker,
            (((0,), (0,)), ((), ())),
            preferred_element_type=jnp.float32,
        )


def active(ranges, offset, lag, band):
    base = lag * band + 1
    first = jnp.clip(ranges[0, offset] - base, 0, band)
    last = jnp.clip(ranges[0, NEAR + offset] - base, 0, band)
    return first, last


def history_terms(ranges, slots, sizes, shots, rows, blocks, stage, arrive, emitted):
    _, width, tile_len = stage.shape
    band = blocks.shape[1]
    lag = lax.axis_index("lag")
    offsets = slot_offsets(lax.axis_index("patch"))

    def window(k):
        return rows[pl.ds(pl.multiple_of((band - 1 - k) * shots, shots), width), :]

    def one_slot(index, carry):
        offset = offsets[slots[-1]]
        for i, slot in enumerate(slots[:-1]):
            offset = jnp.where(index == i, offsets[slot], offset)
        first, last = active(ranges, offset, lag, band)
        arrive(index, first, last, offset)

        def emit(total):
            stage[index] = total.astype(jnp.bfloat16)
            emitted(index, total)

        def branch(size):
            def run():
                start = jnp.minimum(first, band - size)
                left, right = [], []
                for i in range(size):
                    k = start + i
                    live = (k >= first) & (k < last)
                    tile = blocks[index, k]
                    left.append(window(k))
                    right.append(jnp.where(live, tile, jnp.zeros_like(tile)))
                emit(dot(jnp.concatenate(left, axis=1), jnp.concatenate(right, axis=0)))

            return run

        count = last - first
        which = jnp.where(count > 0, 1, 0)
        for i, size in enumerate(sizes[:-1]):
            which = jnp.where(count > size, i + 2, which)
        lax.switch(
            which,
            [lambda: emit(jnp.zeros((width, tile_len), jnp.float32))]
            + [branch(size) for size in sizes],
        )
        return carry

    lax.fori_loop(0, len(slots), one_slot, None)


def transposed(rows, history, rim, steps):
    band, _, shots = history.shape
    tile_len = rows.shape[1]
    lag = lax.axis_index("lag")
    for k in range(band):
        rows[(band - 1 - k) * shots : (band - k) * shots, :] = history[k].T

    @pl.when(lag > 0)
    def _():
        for k in range(steps - 1):
            at = (band + steps - 2 - k) * shots
            rows[at : at + shots, :] = rim[k].T

    @pl.when(lag == 0)
    def _():
        rows[band * shots :, :] = jnp.zeros(((steps - 1) * shots, tile_len), jnp.bfloat16)


def fetcher(ranges, slots, weights, blocks, sems):
    band, tile_len = blocks.shape[1:3]
    lag = lax.axis_index("lag")
    offsets = slot_offsets(lax.axis_index("patch"))

    def fetch(index, offset, k):
        columns = pl.ds(pl.multiple_of(offset * tile_len, tile_len), tile_len)
        return pltpu.make_async_copy(
            weights.at[k, :, columns], blocks.at[index, k], sems.at[index, k]
        )

    def fetch_all():
        for index, slot in enumerate(slots):
            first, last = active(ranges, offsets[slot], lag, band)
            lax.fori_loop(
                first, last, lambda k, c, i=index, o=offsets[slot]: fetch(i, o, k).start(), None
            )

    def arrive(index, first, last, offset):
        lax.fori_loop(first, last, lambda k, c: fetch(index, offset, k).wait(), None)

    return fetch_all, arrive


def far_kernel(steps, sizes, ranges, rim, history_hbm, weights, *refs):
    far_message, odd_message, stage = refs[:3]
    rows, blocks, history, sems, keep_sem, out_sems = refs[3:]
    shots = history.shape[2]

    held = pltpu.make_async_copy(history_hbm, history, keep_sem)
    held.start()
    fetch_all, arrive = fetcher(ranges, range(FIRST), weights, blocks, sems)
    fetch_all()
    held.wait()
    transposed(rows, history, rim, steps)

    targets = (far_message, odd_message)

    def send(index):
        return pltpu.make_async_copy(
            stage.at[index, pl.ds(0, shots)], targets[index], out_sems.at[index]
        )

    def emitted(index, total):
        for i in range(FIRST):
            pl.when(index == i)(lambda i=i: send(i).start())

    history_terms(ranges, range(FIRST), sizes, shots, rows, blocks, stage, arrive, emitted)
    for index in range(FIRST):
        send(index).wait()


def near_kernel(steps, sizes, ranges, rim, far_stage, history_hbm, weights, *refs):
    near_message, core_message, own, stage, rest, recent = refs[:6]
    rows, blocks, history, sems, keep_sems, out_sems = refs[6:]
    past = pltpu.make_async_copy(history_hbm, history, keep_sems.at[1])
    past.start()
    fetch_all, arrive = fetcher(ranges, range(FIRST, NEAR), weights, blocks, sems)
    fetch_all()
    held = pltpu.make_async_copy(weights.at[pl.ds(0, recent.shape[0])], recent, keep_sems.at[0])
    held.start()
    shots = own.shape[0]
    targets = (near_message, core_message)

    def pass_on(slot):
        held = far_stage.at[slot] if slot < FIRST else stage.at[slot - FIRST]
        return pltpu.make_async_copy(
            held.at[pl.ds(shots, shots)], rest.at[pl.ds(slot * shots, shots)], out_sems.at[0, slot]
        )

    def send(index):
        return pltpu.make_async_copy(
            stage.at[index, pl.ds(0, shots)], targets[index], out_sems.at[1, index]
        )

    for slot in range(FIRST):
        pass_on(slot).start()

    def emitted(index, total):
        for i in range(NEAR - FIRST):

            @pl.when(index == i)
            def _(i=i):
                pass_on(FIRST + i).start()
                if i < len(targets):
                    send(i).start()
                else:
                    own[...] = total[:shots]

    past.wait()
    transposed(rows, history, rim, steps)
    history_terms(
        ranges, range(FIRST, NEAR), sizes, shots, rows, blocks, stage, arrive, emitted
    )
    held.wait()
    for slot in range(NEAR):
        pass_on(slot).wait()
    for index in range(len(targets)):
        send(index).wait()


def sum_kernel(own, *refs):
    blocks, (total_ref, half) = refs[:-2], refs[-2:]
    total = own[...]
    for block in blocks:
        total = total + block[...].astype(jnp.float32)
    total_ref[...] = total
    half[...] = total.astype(jnp.bfloat16)


def step_kernel(step, last_step, ranges, source, inverse, own, *refs):
    shots, tile_len = own.shape
    refs = list(refs)
    received = [refs.pop(0) for _ in range(NEAR - 1 if step > 0 else 0)]
    total = own[...]
    for block in received:
        total = total + block[...].astype(jnp.float32)
    known = source.shape[0] // shots
    right = source[step * shots : (step + 1) * shots, :] - total if step < known else -total
    if step != 1:
        right = right - refs.pop(0)[...].astype(jnp.float32)
    density = dot(right.astype(jnp.bfloat16), inverse[...])
    rounded = density.astype(jnp.bfloat16)
    if last_step:
        refs[0][...] = rounded
        return
    weights, far_stage, near_stage = refs[:3]
    rest_far = refs[3] if step == 0 else None
    refs = refs[4 if step == 0 else 3 :]
    olders, outs = refs[:step], refs[step:]
    cross, next_own = outs[:2]
    messages = outs[2 : NEAR + 1]
    band_zero = lax.axis_index("lag") == 0
    for density_ref in outs[NEAR + 1 :]:
        density_ref[...] = rounded
    if step + 1 >= known:
        at = (step + 1 - known) * shots
        carried = jnp.where(lax.axis_index("lag") == 1, source[at : at + shots, :], 0.0)
        total = total - carried
    cross[...] = jnp.where(band_zero, density, total).astype(jnp.bfloat16)
    recent = [rounded] + [ref[...] for ref in olders]
    steps = far_stage.shape[1] // shots
    ahead = jnp.where(band_zero, step + 1, min(step + 2, steps - 1))
    rows = pl.ds(pl.multiple_of(ahead * shots, shots), shots)
    for slot, offset in enumerate(slot_offsets(lax.axis_index("patch"))):
        held = far_stage.at[slot] if slot < FIRST else near_stage.at[slot - FIRST]
        terms = held[rows, :].astype(jnp.float32)
        if step == 0:
            there = rest_far[slot * shots : (slot + 1) * shots, :].astype(jnp.float32)
            terms = terms + jnp.where(band_zero, there, 0.0)
        columns = pl.ds(pl.multiple_of(offset * tile_len, tile_len), tile_len)
        for k, block in enumerate(recent):
            lag = k + 1
            live = band_zero & (ranges[0, offset] <= lag) & (lag < ranges[0, NEAR + offset])
            scale = jnp.where(live, 1.0, 0.0).astype(jnp.float32)
            terms = terms + scale * dot(block, weights[k, :, columns])
        if slot < NEAR - 1:
            messages[slot][...] = terms.astype(jnp.bfloat16)
        else:
            next_own[...] = terms


def begin_kernel(near_lags, *refs):
    count = (len(refs) - 3) // 2
    mine, far, (out, rows, sem) = refs[:count], refs[count : 2 * count], refs[2 * count :]
    keeps = lax.axis_index("lag") < near_lags
    for k in range(count):
        block = jnp.where(keeps, mine[k][...], far[k][...])
        rows[k] = block.astype(jnp.float32).T.astype(jnp.bfloat16)
    copy = pltpu.make_async_copy(rows, out.at[pl.ds(0, count)], sem)
    copy.start()
    copy.wait()


def finish_kernel(near_lags, begun, mine, far, out, rows, sem):
    del begun
    block = jnp.where(lax.axis_index("lag") < near_lags, mine[...], far[...])
    rows[...] = block.astype(jnp.float32).T.astype(jnp.bfloat16)
    copy = pltpu.make_async_copy(rows, out.at[out.shape[0] - 1], sem)
    copy.start()
    copy.wait()


def call(kernel, outs, specs, scratch=(), out_specs=None, aliases=None, limit=8 << 20):
    made = []
    for shape, dtype, *space in outs:
        made.append(space[0](shape, dtype) if space else jax.ShapeDtypeStruct(shape, dtype))
    return pl.pallas_call(
        kernel,
        out_shape=made,
        in_specs=[pl.BlockSpec(memory_space=space) for space in specs],
        out_specs=[pl.BlockSpec(memory_space=s) for s in (out_specs or [VMEM] * len(made))],
        scratch_shapes=list(scratch),
        input_output_aliases=aliases or {},
        compiler_params=pltpu.CompilerParams(vmem_limit_bytes=limit),
    )


def near_memory(array):
    return pltpu.with_memory_space_constraint(array, VMEM)


def far_memory(array):
    return pltpu.with_memory_space_constraint(array, pltpu.HBM)


def lag_partners(lags, distance):
    return [(i, i ^ distance) for i in range(lags)]


def lag_sum(block, lags):
    far, distance = None, 1
    while distance < lags:
        if far is not None:
            block = block + far.astype(block.dtype)
        far = lax.ppermute(block.astype(jnp.bfloat16), "lag", lag_partners(lags, distance))
        distance *= 2
    return block, far


def from_band_zero(block, lags):
    index = lax.axis_index("lag")
    distance = 1
    far = block
    while distance < lags:
        if distance > 1:
            block = jnp.where(index < distance // 2, block, far)
        far = lax.ppermute(block, "lag", lag_partners(lags, distance))
        distance *= 2
    return block, far


def local(interaction, history, near_inverse, lag_ranges, receiver_tile, receiver_panel, residuals):
    tile_len = near_inverse.shape[1]
    band, _, shots = history.shape
    recv, steps, _ = residuals.shape
    patches, lags = lax.axis_size("patch"), lax.axis_size("lag")
    width = steps * shots
    f32, bf16 = jnp.float32, jnp.bfloat16
    block = (shots, tile_len)
    routes = pairings(patches)
    piece = width // PIECES

    rim = lax.ppermute(
        history[band - steps + 1 :], "lag", [(i, (i + 1) % lags) for i in range(lags)]
    )
    (outgoing,) = call(
        pack_kernel,
        [((patches * CAP, piece + LANES), bf16, pltpu.HBM)],
        [pltpu.HBM] * 2 + [VMEM],
        [VMEM((1, recv), jnp.int32)] * 2 + [pltpu.SemaphoreType.DMA((2,))]
        + [VMEM((patches * CAP, piece + LANES), bf16), pltpu.SemaphoreType.DMA],
        out_specs=[pltpu.HBM],
    )(
        far_memory(receiver_tile.reshape(1, recv)),
        far_memory(receiver_panel.reshape(1, recv)),
        residuals.reshape(recv, width),
    )
    arrived = lax.all_to_all(
        outgoing.reshape(patches, CAP, piece + LANES),
        "patch",
        split_axis=0,
        concat_axis=0,
        tiled=True,
    ).reshape(patches * CAP, piece + LANES)
    (source,) = call(
        functools.partial(source_kernel, shots), [((piece, tile_len), f32, VMEM)], [VMEM]
    )(arrived)
    source = near_memory(source)

    sizes = [*range(2, band, 2), band]
    older_rows = ((band + steps - 1) * shots, tile_len)
    *first, far_stage = call(
        functools.partial(far_kernel, steps, sizes),
        [(block, bf16, pltpu.HBM)] * FIRST
        + [((FIRST, width, tile_len), bf16, VMEM)],
        [pltpu.SMEM, VMEM] + [pltpu.HBM] * 2,
        [
            VMEM(older_rows, bf16),
            VMEM((FIRST, band, tile_len, tile_len), bf16),
            VMEM((band, tile_len, shots), bf16),
            pltpu.SemaphoreType.DMA((FIRST, band)),
            pltpu.SemaphoreType.DMA,
            pltpu.SemaphoreType.DMA((FIRST,)),
        ],
        out_specs=[pltpu.HBM] * FIRST + [VMEM],
        limit=FAR_LIMIT,
    )(far_memory(lag_ranges), far_memory(rim), far_memory(history), far_memory(interaction))
    far_stage = near_memory(far_stage)
    *second, own, near_stage, rest, recent = call(
        functools.partial(near_kernel, steps, sizes),
        [(block, bf16, pltpu.HBM)] * (NEAR - 1 - FIRST)
        + [
            (block, f32, VMEM),
            ((NEAR - FIRST, width, tile_len), bf16, VMEM),
            ((NEAR * shots, tile_len), bf16, pltpu.HBM),
            ((steps - 1, tile_len, NEAR * tile_len), bf16, VMEM),
        ],
        [pltpu.SMEM] + [VMEM] * 2 + [pltpu.HBM] * 2,
        [
            VMEM(older_rows, bf16),
            VMEM((NEAR - FIRST, band, tile_len, tile_len), bf16),
            VMEM((band, tile_len, shots), bf16),
            pltpu.SemaphoreType.DMA((NEAR - FIRST, band)),
            pltpu.SemaphoreType.DMA((2,)),
            pltpu.SemaphoreType.DMA((2, NEAR)),
        ],
        out_specs=[pltpu.HBM] * (NEAR - 1 - FIRST) + [VMEM] * 2 + [pltpu.HBM, VMEM],
        limit=NEAR_LIMIT,
    )(far_memory(lag_ranges), far_memory(rim), far_stage, far_memory(history), far_memory(interaction))
    near_stage, recent = near_memory(near_stage), near_memory(recent)
    messages = [*first, *second]

    def exchange(blocks):
        gone = []
        for b, r in zip(blocks, routes):
            gone.append(lax.ppermute(b, "patch", r))
        return gone

    own, half = call(
        sum_kernel, [(block, f32, pltpu.HBM), (block, bf16)], [VMEM] * NEAR
    )(near_memory(own), *exchange(messages))
    if lags == 2:
        own, far = far_memory(own), lax.ppermute(half, "lag", lag_partners(lags, 1))
    else:
        own, far = lag_sum(own, lags)
    here, there = lag_sum(rest, lags)
    if lags > 2:
        there = there + (here - rest)

    def cross_bands(block):
        if lags == 2:
            swapped = lax.ppermute(block, "lag", lag_partners(lags, 1))
            return (block, swapped), swapped
        outward = from_band_zero(block, lags)
        inward, last = lag_sum(jnp.where(lax.axis_index("lag") > 0, block, 0), lags)
        return outward, inward + last

    densities, outward, inward, received = [], [], [far], []
    for step in range(steps):
        last_step = step == steps - 1
        inputs = [lag_ranges, source, near_inverse if step else far_memory(near_inverse), own, *received]
        if step != 1:
            inputs.append(inward[max(step - 1, 0)])
        outs = [(block, bf16)]
        if not last_step:
            inputs += [recent, far_stage, near_stage] + [there] * (step == 0) + densities[::-1]
            outs = [(block, bf16), (block, f32, VMEM)] + [(block, bf16)] * (NEAR - 1)
            outs += [(block, bf16, VMEM)] * (step < steps - 2)
        results = call(
            functools.partial(step_kernel, step, last_step),
            outs,
            [pltpu.SMEM] + [VMEM] * (len(inputs) - 1),
        )(*inputs)
        if last_step:
            ends, _ = cross_bands(results[0])
        else:
            densities += [near_memory(r) for r in results[NEAR + 1 :]]
            sent, back = cross_bands(results[0])
            outward.append(sent)
            if step == 0:
                inward = [far]
            else:
                inward.append(back)
            own = near_memory(results[1])
            received = exchange(results[2 : NEAR + 1])
    whole = ((steps, tile_len, shots), bf16)
    pairs = [mine for mine, _ in outward] + [theirs for _, theirs in outward]
    (begun,) = call(
        functools.partial(begin_kernel, lags // 2),
        [whole],
        [VMEM] * len(pairs),
        [VMEM((steps - 1, tile_len, shots), bf16), pltpu.SemaphoreType.DMA],
        out_specs=[pl.ANY],
    )(*pairs)
    (out,) = call(
        functools.partial(finish_kernel, lags // 2),
        [whole],
        [pl.ANY, VMEM, VMEM],
        [VMEM((tile_len, shots), bf16), pltpu.SemaphoreType.DMA],
        out_specs=[pl.ANY],
        aliases={0: 0},
    )(begun, *ends)
    return out


def solution(mesh):
    in_specs = (
        P("lag", "patch", None),
        P("lag", "patch", None),
        P("patch", None),
        P("patch", None),
        P("patch", None),
        P("patch"),
        P("patch", None, None),
    )
    out_specs = P(None, "patch", None)

    return jax.shard_map(local, mesh=mesh, in_specs=in_specs, out_specs=out_specs, check_vma=False)
```

```python
import functools

import jax
import jax.numpy as jnp
from jax import lax
from jax.experimental import pallas as pl
from jax.experimental.pallas import tpu as pltpu
from jax.sharding import PartitionSpec as P

NEAR = 5
CAP = 16
HALF = NEAR // 2
LANES = 128
VMEM = pltpu.VMEM


def dot(left, right):
    return jnp.dot(left, right, preferred_element_type=jnp.float32)


def slot_offsets(patch):
    odd = lax.rem(patch, 2)
    high = lax.rem(lax.div(patch, 2), 2)
    return [4 * high, 1 + 2 * odd, 4 - 4 * high, 3 - 2 * odd, HALF]


def pairings(patches):
    far = [(i + 2 if i & 2 else i - 2) % patches for i in range(patches)]
    odd_even = [(i + 1 if i & 1 else i - 1) % patches for i in range(patches)]
    near = [i ^ 2 for i in range(patches)]
    core = [i ^ 1 for i in range(patches)]
    return [list(enumerate(p)) for p in (far, odd_even, near, core)]


def pack_kernel(tile_hbm, panel_hbm, history, rows_ref, out_ref, edge, tile_ref, panel_ref, sems):
    copies = [
        pltpu.make_async_copy(tile_hbm, tile_ref, sems.at[0]),
        pltpu.make_async_copy(panel_hbm, panel_ref, sems.at[1]),
        pltpu.make_async_copy(
            history.at[pl.ds(history.shape[0] - edge.shape[0], edge.shape[0])], edge, sems.at[2]
        ),
    ]
    for copy in copies:
        copy.start()
    for copy in copies[:2]:
        copy.wait()
    recv = rows_ref.shape[0]
    width = rows_ref.shape[1]
    slots = out_ref.shape[0]
    patches = slots // CAP
    tile = tile_ref[...]
    hot = lax.broadcasted_iota(jnp.int32, (patches, recv), 0) == tile
    before = lax.broadcasted_iota(jnp.int32, (recv, recv), 0) < lax.broadcasted_iota(
        jnp.int32, (recv, recv), 1
    )
    hot = jnp.where(hot, 1.0, 0.0)
    ahead = dot(hot.astype(jnp.bfloat16), jnp.where(before, 1.0, 0.0).astype(jnp.bfloat16))
    earlier = jnp.sum(hot * ahead, axis=0, keepdims=True).astype(jnp.int32)
    slot = tile * CAP + earlier
    placed = lax.broadcasted_iota(jnp.int32, (slots, recv), 0) == slot
    placer = jnp.where(placed, 1.0, 0.0).astype(jnp.bfloat16)
    out_ref[:, :width] = dot(placer, rows_ref[...]).astype(jnp.bfloat16)
    marks = jnp.where(placed, (panel_ref[...] + 1).astype(jnp.float32), 0.0)
    label = jnp.sum(marks, axis=1, keepdims=True)
    out_ref[:, width:] = jnp.broadcast_to(label, (slots, LANES)).astype(jnp.bfloat16)
    copies[2].wait()


def source_kernel(arrived_ref, *outs):
    slots = arrived_ref.shape[0]
    shots, tile_len = outs[0].shape
    width = len(outs) * shots
    label = arrived_ref[:, width:].astype(jnp.float32)
    lane = lax.broadcasted_iota(jnp.int32, (slots, LANES), 1)
    picker = jnp.concatenate(
        [
            jnp.where(label == (lane + (1 + first)).astype(jnp.float32), 1.0, 0.0)
            for first in range(0, tile_len, LANES)
        ],
        axis=1,
    ).astype(jnp.bfloat16)
    for step, out in enumerate(outs):
        out[...] = lax.dot_general(
            arrived_ref[:, step * shots : (step + 1) * shots],
            picker,
            (((0,), (0,)), ((), ())),
            preferred_element_type=jnp.float32,
        )


def older_kernel(steps, sizes, ranges, rim, history, inverse_hbm, weights, *refs):
    outs, (rows, blocks, sems, out_sems) = refs[:-4], refs[-4:]
    messages, outs = outs[: NEAR - 1], outs[NEAR - 1 :]
    own, stage, recent, inverse = outs[:4]
    (rest,) = outs[4:]
    band, tile_len, shots = history.shape
    lag = lax.axis_index("lag")
    offsets = slot_offsets(lax.axis_index("patch"))

    def bounds(offset):
        base = lag * band + 1
        first = jnp.clip(ranges[0, offset] - base, 0, band)
        last = jnp.clip(ranges[0, NEAR + offset] - base, 0, band)
        return first, last

    def fetch(slot, offset, k):
        columns = pl.ds(pl.multiple_of(offset * tile_len, tile_len), tile_len)
        return pltpu.make_async_copy(
            weights.at[k, :, columns], blocks.at[slot, k], sems.at[slot, k]
        )

    def send(slot, step, target):
        return pltpu.make_async_copy(
            stage.at[slot, pl.ds(step * shots, shots)], target, out_sems.at[slot, step]
        )

    for slot, offset in enumerate(offsets):
        first, last = bounds(offset)
        lax.fori_loop(first, last, lambda k, c, s=slot, o=offset: fetch(s, o, k).start(), None)
    keep = [
        pltpu.make_async_copy(weights.at[pl.ds(0, steps - 1)], recent, out_sems.at[NEAR, 0]),
        pltpu.make_async_copy(inverse_hbm, inverse, out_sems.at[NEAR, 1]),
    ]
    for copy in keep:
        copy.start()
    for k in range(band):
        rows[(band - 1 - k) * shots : (band - k) * shots, :] = history[k].T

    @pl.when(lag > 0)
    def _():
        for k in range(steps - 1):
            at = (band + steps - 2 - k) * shots
            rows[at : at + shots, :] = rim[k].T

    @pl.when(lag == 0)
    def _():
        rows[band * shots :, :] = jnp.zeros(((steps - 1) * shots, tile_len), jnp.bfloat16)

    def window(k):
        return rows[pl.ds(pl.multiple_of((band - 1 - k) * shots, shots), steps * shots), :]

    def one_slot(slot, carry):
        offset = offsets[-1]
        for j in range(NEAR - 1):
            offset = jnp.where(slot == j, offsets[j], offset)
        first, last = bounds(offset)
        lax.fori_loop(first, last, lambda k, c: fetch(slot, offset, k).wait(), None)

        def emit(total):
            stage[slot] = total.astype(jnp.bfloat16)

            @pl.when(slot == NEAR - 1)
            def _():
                own[...] = total[:shots]

        def branch(size):
            def run():
                start = jnp.minimum(first, band - size)
                left, right = [], []
                for i in range(size):
                    k = start + i
                    live = (k >= first) & (k < last)
                    tile = blocks[slot, k]
                    left.append(window(k))
                    right.append(jnp.where(live, tile, jnp.zeros_like(tile)))
                emit(dot(jnp.concatenate(left, axis=1), jnp.concatenate(right, axis=0)))

            return run

        count = last - first
        which = jnp.where(count > 0, 1, 0)
        for i, size in enumerate(sizes[:-1]):
            which = jnp.where(count > size, i + 2, which)
        lax.switch(
            which,
            [lambda: emit(jnp.zeros((steps * shots, tile_len), jnp.float32))]
            + [branch(size) for size in sizes],
        )
        for j in range(NEAR - 1):
            pl.when(slot == j)(lambda j=j: send(j, 0, messages[j]).start())
        send(slot, 1, rest.at[pl.ds(slot * shots, shots)]).start()
        return carry

    lax.fori_loop(0, NEAR, one_slot, None)
    for copy in keep:
        copy.wait()
    for slot in range(NEAR):
        if slot < NEAR - 1:
            send(slot, 0, messages[slot]).wait()
        send(slot, 1, rest.at[pl.ds(slot * shots, shots)]).wait()


def step_kernel(step, last_step, ranges, source, inverse, own, *refs):
    shots, tile_len = own.shape
    refs = list(refs)
    received = [refs.pop(0) for _ in range(NEAR - 1 if step > 0 else 0)]
    total = own[...]
    for block in received:
        total = total + block[...].astype(jnp.float32)
    right = source[...] - total
    if step != 1:
        right = right - refs.pop(0)[...].astype(jnp.float32)
    density = dot(right.astype(jnp.bfloat16), inverse[...])
    rounded = density.astype(jnp.bfloat16)
    if last_step:
        refs[0][...] = rounded
        return
    weights, stage = refs[:2]
    rest_far = refs[2] if step == 0 else None
    refs = refs[3 if step == 0 else 2 :]
    olders, outs = refs[:step], refs[step:]
    cross, next_own = outs[:2]
    messages = outs[2 : NEAR + 1]
    band_zero = lax.axis_index("lag") == 0
    for density_ref in outs[NEAR + 1 :]:
        density_ref[...] = rounded
    cross[...] = jnp.where(band_zero, density, total).astype(jnp.bfloat16)
    recent = [rounded] + [ref[...] for ref in olders]
    steps = stage.shape[1] // shots
    ahead = jnp.where(band_zero, step + 1, min(step + 2, steps - 1))
    rows = pl.ds(pl.multiple_of(ahead * shots, shots), shots)
    for slot, offset in enumerate(slot_offsets(lax.axis_index("patch"))):
        terms = stage[slot, rows, :].astype(jnp.float32)
        if step == 0:
            there = rest_far[slot * shots : (slot + 1) * shots, :].astype(jnp.float32)
            terms = terms + jnp.where(band_zero, there, 0.0)
        columns = pl.ds(pl.multiple_of(offset * tile_len, tile_len), tile_len)
        for k, block in enumerate(recent):
            lag = k + 1
            live = band_zero & (ranges[0, offset] <= lag) & (lag < ranges[0, NEAR + offset])
            scale = jnp.where(live, 1.0, 0.0).astype(jnp.float32)
            terms = terms + scale * dot(block, weights[k, :, columns])
        if slot < NEAR - 1:
            messages[slot][...] = terms.astype(jnp.bfloat16)
        else:
            next_own[...] = terms


def begin_kernel(near_lags, *refs):
    count = (len(refs) - 3) // 2
    mine, far, (out, rows, sem) = refs[:count], refs[count : 2 * count], refs[2 * count :]
    keeps = lax.axis_index("lag") < near_lags
    for k in range(count):
        block = jnp.where(keeps, mine[k][...], far[k][...])
        rows[k] = block.astype(jnp.float32).T.astype(jnp.bfloat16)
    copy = pltpu.make_async_copy(rows, out.at[pl.ds(0, count)], sem)
    copy.start()
    copy.wait()


def finish_kernel(near_lags, begun, mine, far, out, rows, sem):
    del begun
    block = jnp.where(lax.axis_index("lag") < near_lags, mine[...], far[...])
    rows[...] = block.astype(jnp.float32).T.astype(jnp.bfloat16)
    copy = pltpu.make_async_copy(rows, out.at[out.shape[0] - 1], sem)
    copy.start()
    copy.wait()


def call(kernel, outs, specs, scratch=(), out_specs=None, aliases=None, limit=8 << 20):
    made = []
    for shape, dtype, *space in outs:
        made.append(space[0](shape, dtype) if space else jax.ShapeDtypeStruct(shape, dtype))
    return pl.pallas_call(
        kernel,
        out_shape=made,
        in_specs=[pl.BlockSpec(memory_space=space) for space in specs],
        out_specs=[pl.BlockSpec(memory_space=s) for s in (out_specs or [VMEM] * len(made))],
        scratch_shapes=list(scratch),
        input_output_aliases=aliases or {},
        compiler_params=pltpu.CompilerParams(vmem_limit_bytes=limit),
    )


def near_memory(array):
    return pltpu.with_memory_space_constraint(array, VMEM)


def far_memory(array):
    return pltpu.with_memory_space_constraint(array, pltpu.HBM)


def lag_partners(lags, distance):
    return [(i, i ^ distance) for i in range(lags)]


def lag_sum(block, lags):
    far, distance = None, 1
    while distance < lags:
        if far is not None:
            block = block + far.astype(block.dtype)
        far = lax.ppermute(block.astype(jnp.bfloat16), "lag", lag_partners(lags, distance))
        distance *= 2
    return block, far


def from_band_zero(block, lags):
    index = lax.axis_index("lag")
    distance = 1
    far = block
    while distance < lags:
        if distance > 1:
            block = jnp.where(index < distance // 2, block, far)
        far = lax.ppermute(block, "lag", lag_partners(lags, distance))
        distance *= 2
    return block, far


def local(interaction, history, near_inverse, lag_ranges, receiver_tile, receiver_panel, residuals):
    tile_len = near_inverse.shape[1]
    band, _, shots = history.shape
    recv, steps, _ = residuals.shape
    patches, lags = lax.axis_size("patch"), lax.axis_size("lag")
    width = steps * shots
    f32, bf16 = jnp.float32, jnp.bfloat16
    block = (shots, tile_len)
    routes = pairings(patches)

    outgoing, edge = call(
        pack_kernel,
        [((patches * CAP, width + LANES), bf16), ((steps - 1, tile_len, shots), bf16)],
        [pltpu.HBM] * 3 + [VMEM],
        [VMEM((1, recv), jnp.int32)] * 2 + [pltpu.SemaphoreType.DMA((3,))],
        out_specs=[VMEM, pl.ANY],
    )(
        far_memory(receiver_tile.reshape(1, recv)),
        far_memory(receiver_panel.reshape(1, recv)),
        far_memory(history),
        residuals.reshape(recv, width),
    )
    rim = lax.ppermute(edge, "lag", [(i, (i + 1) % lags) for i in range(lags)])
    arrived = lax.all_to_all(
        outgoing.reshape(patches, CAP, width + LANES),
        "patch",
        split_axis=0,
        concat_axis=0,
        tiled=True,
    ).reshape(patches * CAP, width + LANES)
    source = call(source_kernel, [(block, f32, VMEM)] * steps, [VMEM])(arrived)
    source = [near_memory(s) for s in source]

    sizes = [*range(1, band + 1)]
    older = call(
        functools.partial(older_kernel, steps, sizes),
        [(block, bf16)] * (NEAR - 1)
        + [
            (block, f32, VMEM),
            ((NEAR, width, tile_len), bf16, VMEM),
            ((steps - 1, tile_len, NEAR * tile_len), bf16, VMEM),
            ((tile_len, tile_len), bf16, VMEM),
        ]
        + [((NEAR * shots, tile_len), bf16)],
        [pltpu.SMEM, VMEM, VMEM, pltpu.HBM, pltpu.HBM],
        [
            VMEM(((band + steps - 1) * shots, tile_len), bf16),
            VMEM((NEAR, band, tile_len, tile_len), bf16),
            pltpu.SemaphoreType.DMA((NEAR, band)),
            pltpu.SemaphoreType.DMA((NEAR + 1, steps)),
        ],
        out_specs=[pl.ANY] * (NEAR - 1) + [VMEM] * 4 + [pl.ANY],
        limit=54 << 20,
    )(lag_ranges, rim, history, far_memory(near_inverse), far_memory(interaction))
    messages, (own, stage, recent, inverse, rest) = older[: NEAR - 1], older[NEAR - 1 :]
    stage, recent, inverse = near_memory(stage), near_memory(recent), near_memory(inverse)

    def exchange(blocks):
        gone = []
        for b, r in zip(blocks, routes):
            gone.append(lax.ppermute(b, "patch", r))
        return gone

    for incoming in exchange(messages):
        own = own + incoming.astype(f32)
    own, far = lag_sum(own, lags)
    here, there = lag_sum(rest, lags)
    if lags > 2:
        there = there + (here - rest)

    def cross_bands(block):
        if lags == 2:
            swapped = lax.ppermute(block, "lag", lag_partners(lags, 1))
            return (block, swapped), swapped
        outward = from_band_zero(block, lags)
        inward, last = lag_sum(jnp.where(lax.axis_index("lag") > 0, block, 0), lags)
        return outward, inward + last

    densities, outward, inward = [], [], [far]
    received = []
    for step in range(steps):
        last_step = step == steps - 1
        inputs = [lag_ranges, source[step], inverse, own, *received]
        if step != 1:
            inputs.append(inward[max(step - 1, 0)])
        outs = [(block, bf16)]
        if not last_step:
            inputs += [recent, stage] + [there] * (step == 0) + densities[::-1]
            outs = [(block, bf16), (block, f32, VMEM)] + [(block, bf16)] * (NEAR - 1)
            outs += [(block, bf16, VMEM)] * (step < steps - 2)
        results = call(
            functools.partial(step_kernel, step, last_step),
            outs,
            [pltpu.SMEM] + [VMEM] * (len(inputs) - 1),
        )(*inputs)
        if last_step:
            ends, _ = cross_bands(results[0])
        else:
            densities += [near_memory(r) for r in results[NEAR + 1 :]]
            sent, back = cross_bands(results[0])
            outward.append(sent)
            if step == 0:
                inward = [far]
            else:
                inward.append(back)
            own = near_memory(results[1])
            received = exchange(results[2 : NEAR + 1])
    whole = ((steps, tile_len, shots), bf16)
    pairs = [mine for mine, _ in outward] + [theirs for _, theirs in outward]
    (begun,) = call(
        functools.partial(begin_kernel, lags // 2),
        [whole],
        [VMEM] * len(pairs),
        [VMEM((steps - 1, tile_len, shots), bf16), pltpu.SemaphoreType.DMA],
        out_specs=[pl.ANY],
    )(*pairs)
    (out,) = call(
        functools.partial(finish_kernel, lags // 2),
        [whole],
        [pl.ANY, VMEM, VMEM],
        [VMEM((tile_len, shots), bf16), pltpu.SemaphoreType.DMA],
        out_specs=[pl.ANY],
        aliases={0: 0},
    )(begun, *ends)
    return out


def solution(mesh):
    in_specs = (
        P("lag", "patch", None),
        P("lag", "patch", None),
        P("patch", None),
        P("patch", None),
        P("patch", None),
        P("patch"),
        P("patch", None, None),
    )
    out_specs = P(None, "patch", None)

    return jax.shard_map(local, mesh=mesh, in_specs=in_specs, out_specs=out_specs, check_vma=False)
```
